128 devices in a mesh: ctx: 16 (over x, z), head: 8 (over y, core).
Axes of the slice: x: 4, y: 4, z: 4, core: 2. Of those that a mesh axis runs over, the one named last changes fastest.
Arguments:
- queries: bfloat16 [8192, 8192], P('ctx', 'head'), may hold values from -6 to 6
- key_rows: bfloat16 [8192, 8192], P('ctx', 'head'), may hold values from -8 to 8
- value_rows: bfloat16 [8192, 8192], P('ctx', 'head'), may hold values from -6 to 6
- log_decay: float32 [8192, 64], P('ctx', 'head'), may hold values from -3 to 0, as said below
- write_rate: float32 [8192, 64], P('ctx', 'head'), may hold values from 0 to 1, as said below
- level_weights: float32 [8192, 320], P('ctx', 'head'), may hold values from 0.25 to 2.5
- block_levels: int32 [128], P('ctx'), may hold values from 1 to 5
Outputs:
- mixed: bfloat16 [8192, 8192], P(('ctx', 'head'))
The draws below stay inside these ranges and needn't reach their ends.
Inputs may be any that keep to these rules, and one draw needn't show every extreme that they name: `log_decay`: strictly negative. `write_rate`: strictly positive.
All inputs are finite; a program needn't handle non-finite values.
Results may differ from the reference program's by a relative error of at most 0.0087.
Values may be sent and summed in bfloat16 or wider, within the bound.
A program may use at most 128 MiB of HBM per device.

```python
import math
import jax
import jax.numpy as jnp
from jax import lax

HEAD_TOTAL = 64
D_HEAD = 128
TOK_DEV = 512
BLOCK = 64
LEVELS = 5
TOKEN_TOTAL = 8192
N_CTX = 16


def head_plan(key):
    base_key = jax.random.fold_in(key, 4242)
    share_slow = 0.5
    return jax.random.uniform(jax.random.fold_in(base_key, 1), (HEAD_TOTAL,)) < share_slow


def drawn_plan(key):
    plan_key = jax.random.fold_in(key, 5151)
    block_count = TOKEN_TOTAL // BLOCK
    per_shard = TOK_DEV // BLOCK
    chosen = jax.random.uniform(jax.random.fold_in(plan_key, 1), (block_count,)) < 1.0 / 6.0
    forced = jax.random.randint(jax.random.fold_in(plan_key, 2), (block_count // per_shard,), 0, per_shard)
    block_ids = jnp.arange(block_count)
    forced_hit = block_ids % per_shard == jnp.repeat(forced, per_shard)
    return jnp.logical_or(chosen, forced_hit)


def log_between(key, shape, lower_end, upper_end):
    return jnp.exp(jax.random.uniform(key, shape, jnp.float32, jnp.log(lower_end), jnp.log(upper_end)))


def draw_key_rows(key, part):
    aligned = drawn_plan(key)
    block_count = TOKEN_TOTAL // BLOCK
    feature_count = HEAD_TOTAL * D_HEAD
    shared = jax.random.normal(jax.random.fold_in(key, 31), (block_count, 1, feature_count), jnp.float32)
    noise = jax.random.normal(jax.random.fold_in(key, 32), (block_count, BLOCK, feature_count), jnp.float32)
    values = jnp.where(aligned[:, None, None], shared + 0.5 * noise, noise)
    return jnp.clip(values, -8.0, 8.0).reshape(TOKEN_TOTAL, feature_count).astype(jnp.bfloat16)


def draw_log_decay(key, part):
    slow_heads = head_plan(key)
    slow_rate = log_between(jax.random.fold_in(key, 11), (HEAD_TOTAL,), 0.2, 1.0) / TOKEN_TOTAL
    fast_rate = log_between(jax.random.fold_in(key, 12), (HEAD_TOTAL,), 1.0 / 50.0, 1.0 / 25.0)
    head_decay_rate = jnp.where(slow_heads, slow_rate, fast_rate)
    approximate = log_between(jax.random.fold_in(key, 13), (TOKEN_TOTAL, HEAD_TOTAL), 0.5, 2.0)
    segment_position = jax.random.randint(jax.random.fold_in(key, 14), (4, HEAD_TOTAL), 0, TOKEN_TOTAL)
    segment_length = jax.random.uniform(jax.random.fold_in(key, 15), (4, HEAD_TOTAL), jnp.float32, 0.22, 0.69)
    match_count = jnp.arange(TOKEN_TOTAL)[:, None, None] == segment_position[None]
    segments = jnp.sum(jnp.where(match_count, segment_length[None], 0.0), axis=1)
    return -(head_decay_rate[None, :] * approximate) - segments


def draw_write_rate(key, part):
    slow_heads = head_plan(key)
    aligned = drawn_plan(key)
    block_count = TOKEN_TOTAL // BLOCK
    slow_scale = log_between(jax.random.fold_in(key, 21), (HEAD_TOTAL,), 0.5, 2.0) * 64.0 / TOKEN_TOTAL
    fast_scale = log_between(jax.random.fold_in(key, 22), (HEAD_TOTAL,), 0.1, 0.45)
    head_scale = jnp.where(slow_heads, slow_scale, fast_scale)
    approximate = log_between(jax.random.fold_in(key, 23), (TOKEN_TOTAL, HEAD_TOTAL), 0.5, 2.0)
    base_rate = (head_scale[None, :] * approximate).reshape(block_count, BLOCK, HEAD_TOTAL)
    strong_heads = jax.random.uniform(jax.random.fold_in(key, 24), (block_count, HEAD_TOTAL)) < 0.5
    strong_rate = log_between(jax.random.fold_in(key, 25), (block_count, BLOCK, HEAD_TOTAL), 0.3, 0.9)
    strong_mask = jnp.logical_and(aligned[:, None], strong_heads)
    rate = jnp.where(strong_mask[:, None, :], strong_rate, base_rate)
    return jnp.minimum(rate, 1.0).reshape(TOKEN_TOTAL, HEAD_TOTAL)


def with_ends(entries, own_key, smallest, largest):
    longest = entries.shape.index(max(entries.shape))
    spots = []
    for shift in (0, 1):
        where = [jax.random.randint(jax.random.fold_in(own_key, axis), (), 0, length) for axis, length in enumerate(entries.shape)]
        where[longest] = (where[longest] + shift) % entries.shape[longest]
        spots.append(tuple(where))
    return entries.at[spots[0]].set(smallest).at[spots[1]].set(largest)


def block_scale(own_key, shape, cuts, least, top_value):
    level = 1.0
    for dim, parts in cuts:
        draws = jax.random.uniform(jax.random.fold_in(jax.random.fold_in(own_key, 6), dim), (parts,), jnp.float32, least / len(cuts), top_value / len(cuts))
        level = level * jnp.repeat(jnp.exp(draws), shape[dim] // parts).reshape((-1,) + (1,) * (len(shape) - 1 - dim))
    return level


def gaussian(key, shape, scale, reach, split=(), kind=jnp.bfloat16):
    loudness = block_scale(key, shape, split, -0.22, 0.18) if split else 1.0
    values = jax.random.normal(key, shape, jnp.float32) * scale * loudness
    return jnp.minimum(jnp.maximum(values, -reach), reach).astype(kind)


def setup_inputs(seed: int = 0) -> dict:
    arg_keys = jax.random.split(jax.random.key(seed), 8)
    queries = gaussian(arg_keys[0], (TOKEN_TOTAL, HEAD_TOTAL * D_HEAD), 1.0, 6.0, ((0, 16), (1, 8)))
    key_rows = draw_key_rows(jax.random.fold_in(arg_keys[7], 71), 0)
    value_rows = gaussian(arg_keys[2], (TOKEN_TOTAL, HEAD_TOTAL * D_HEAD), 1.0, 6.0, ((0, 16), (1, 8)))
    log_decay = draw_log_decay(jax.random.fold_in(arg_keys[7], 71), 0)
    write_rate = draw_write_rate(jax.random.fold_in(arg_keys[7], 71), 0)
    level_weights = jnp.clip(jnp.exp(math.log(2.5) - 2.3025851 * jax.random.uniform(arg_keys[5], (TOKEN_TOTAL, HEAD_TOTAL * LEVELS), jnp.float32) ** block_scale(arg_keys[5], (TOKEN_TOTAL, HEAD_TOTAL * LEVELS), ((0, 16), (1, 8)), -0.2, 0.2)), 0.25, 2.5)
    block_levels = with_ends(jax.random.randint(arg_keys[6], (TOKEN_TOTAL // BLOCK,), 1, LEVELS + 1), jax.random.fold_in(arg_keys[6], 1), 1, LEVELS).astype(jnp.int32)
    return dict(queries=queries, key_rows=key_rows, value_rows=value_rows, log_decay=log_decay, write_rate=write_rate, level_weights=level_weights, block_levels=block_levels)


precise = lax.Precision.HIGHEST

def matmul_hi(left_mat, right_mat):
    return jnp.matmul(left_mat, right_mat, precision=precise)

def low_product(form, left_op, right_op):
    return jnp.einsum(form, left_op.astype(jnp.float32), right_op.astype(jnp.float32), precision=precise)

def to_blocks(tensor):
    block_count = tensor.shape[0] // BLOCK
    shaped = tensor.reshape((block_count, BLOCK) + tensor.shape[1:])
    return jnp.moveaxis(shaped, 2, 0)

def prepare(query_in, key_in, value_in, head_count):
    length = query_in.shape[0]
    query_low = query_in.reshape(length, head_count, -1)
    key_f = key_in.astype(jnp.float32).reshape(length, head_count, -1)
    key_low = (key_f * lax.rsqrt(lax.optimization_barrier(jnp.sum(key_f * key_f, axis=-1, keepdims=True)) + 1e-06)).astype(jnp.bfloat16)
    value_f = value_in.astype(jnp.float32).reshape(length, head_count, -1)
    return (query_low, key_low, value_f)

def local_pass(query_low, key_low, value_f, log_decay, write_rate):
    head_count = key_low.shape[1]
    head_width = key_low.shape[2]
    query_b = to_blocks(query_low)
    key_lb = to_blocks(key_low)
    key_b = key_lb.astype(jnp.float32)
    value_b = to_blocks(value_f)
    cum_log = jnp.cumsum(to_blocks(log_decay), axis=-1)
    rate_b = to_blocks(write_rate)
    places = jnp.arange(BLOCK)
    lower_tri = places[:, None] >= places[None, :]
    strict_tri = places[:, None] > places[None, :]
    log_gaps = cum_log[..., :, None] - cum_log[..., None, :]
    decay_incl = jnp.exp(jnp.where(lower_tri, log_gaps, -1e+30))
    decay_strict = jnp.where(strict_tri, decay_incl, 0.0)
    gram_keys = jnp.einsum('hbik,hbjk->hbij', key_b, key_b, precision=precise)
    strict_part = rate_b[..., :, None] * decay_strict * gram_keys
    right_side = jnp.concatenate([rate_b[..., None] * value_b, (rate_b * jnp.exp(cum_log))[..., None] * key_b], axis=-1)
    solved = jax.scipy.linalg.solve_triangular(strict_part, right_side, lower=True, unit_diagonal=True)
    wy_values = solved[..., :head_width]
    wy_keys = solved[..., head_width:]
    inputs = jnp.concatenate([wy_values, jnp.zeros_like(wy_keys)], axis=-1)
    key_tail = jnp.exp(cum_log[..., -1:] - cum_log)[..., None] * key_b
    block_fall = jnp.exp(cum_log[..., -1])
    scores_low = (low_product('hbik,hbjk->hbij', query_b, key_lb) * decay_incl).astype(jnp.bfloat16)
    initial = jnp.concatenate([jnp.zeros((head_count, head_width, head_width), key_b.dtype), jnp.broadcast_to(jnp.eye(head_width, dtype=key_b.dtype), (head_count, head_width, head_width))], axis=-1)

    def advance(carry_state, slices):
        wy_part, given_vals, tail_keys, fall_now = slices
        errors = given_vals - jnp.einsum('hcd,hde->hce', wy_part, carry_state, precision=precise)
        updated = fall_now[:, None, None] * carry_state + jnp.einsum('hcd,hce->hde', tail_keys, errors, precision=precise)
        return (updated, (carry_state, errors))
    end_state, (starts, errors) = lax.scan(advance, initial, (jnp.moveaxis(wy_keys, 1, 0), jnp.moveaxis(inputs, 1, 0), jnp.moveaxis(key_tail, 1, 0), jnp.moveaxis(block_fall, 1, 0)))
    mixed = jnp.exp(cum_log)[..., None] * low_product('hbcd,bhde->hbce', query_b, starts.astype(jnp.bfloat16))
    mixed = mixed + low_product('hbij,bhje->hbie', scores_low, errors.astype(jnp.bfloat16))
    mixed = jnp.moveaxis(mixed, 0, 2).reshape(-1, head_count, 2 * head_width)
    return (mixed, end_state)

def join_runs(left_run, right_run):
    head_width = left_run.shape[-2]
    return matmul_hi(right_run[..., head_width:], left_run) + jnp.concatenate([right_run[..., :head_width], jnp.zeros_like(right_run[..., :head_width])], axis=-1)

def finish(mixed, carried, weights, levels_in):
    length, head_count, twice = mixed.shape
    head_width = twice // 2
    near_part = mixed[..., :head_width]
    row_part = mixed[..., head_width:].astype(jnp.bfloat16)
    far_part = low_product('thd,lhde->thle', row_part, carried.astype(jnp.bfloat16))
    terms = jnp.concatenate([near_part[:, :, None], far_part], axis=2)
    level_ids = jnp.arange(LEVELS)
    keep_mask = (level_ids[None, :] < levels_in[:, None]).astype(weights.dtype)
    scaled = weights.reshape(length // BLOCK, BLOCK, head_count, LEVELS) * keep_mask[:, None, None, :]
    scaled = scaled.reshape(length, head_count, LEVELS)
    total = lax.optimization_barrier(jnp.sum(scaled[..., None] * terms, axis=2))
    return total.astype(jnp.bfloat16).reshape(length, head_count * head_width)

def reference(queries, key_rows, value_rows, log_decay, write_rate, level_weights, block_levels):

    def shard_local(shard_id):
        first = shard_id * TOK_DEV
        query_low, key_low, value_f = prepare(lax.dynamic_slice_in_dim(queries, first, TOK_DEV, 0), lax.dynamic_slice_in_dim(key_rows, first, TOK_DEV, 0), lax.dynamic_slice_in_dim(value_rows, first, TOK_DEV, 0), HEAD_TOTAL)
        return local_pass(query_low, key_low, value_f, lax.dynamic_slice_in_dim(log_decay, first, TOK_DEV, 0), lax.dynamic_slice_in_dim(write_rate, first, TOK_DEV, 0))
    shard_ids = jnp.arange(N_CTX, dtype=jnp.int32)
    mixed_all, run_all = lax.map(shard_local, shard_ids)
    head_width = D_HEAD
    prefix = jnp.broadcast_to(jnp.eye(head_width, dtype=run_all.dtype), run_all.shape[:2] + (head_width, head_width))
    bits_total = N_CTX.bit_length() - 1
    carried = []
    for section in range(bits_total):
        sibling = shard_ids >> section ^ 1
        upper = (shard_ids >> section & 1 == 1)[:, None, None, None]
        other_run = jnp.take(run_all, sibling, axis=0)
        carried.append(jnp.where(upper, matmul_hi(prefix, other_run[..., :head_width]), 0.0))
        prefix = jnp.where(upper, matmul_hi(prefix, other_run[..., head_width:]), prefix)
        if section + 1 < bits_total:
            run_all = join_runs(run_all[0::2], run_all[1::2])
    for section in range(bits_total, LEVELS - 1):
        carried.append(jnp.zeros_like(prefix))
    carried = jnp.stack(carried, axis=1)

    def shard_finish(shard_id):
        first = shard_id * TOK_DEV
        return finish(mixed_all[shard_id], carried[shard_id], lax.dynamic_slice_in_dim(level_weights, first, TOK_DEV, 0), lax.dynamic_slice_in_dim(block_levels, shard_id * (TOK_DEV // BLOCK), TOK_DEV // BLOCK, 0))
    outputs = lax.map(shard_finish, shard_ids)
    return outputs.reshape(TOKEN_TOTAL, HEAD_TOTAL * D_HEAD)
```

```python
import jax
import jax.numpy as jnp
from jax import lax
from jax.experimental import pallas as pl
from jax.experimental.pallas import tpu as pltpu
from jax.sharding import PartitionSpec as P

BLOCK = 64
LEVELS = 5
F32, BF = jnp.float32, jnp.bfloat16
C = 128
NCH = 4
HP = 2
NT = ((1,), (1,))
TN = ((0,), (0,))


def dotf(a, b, dims=((1,), (0,))):
    return lax.dot_general(a, b, (dims, ((), ())), preferred_element_type=F32)


def split(x):
    high = x.astype(BF)
    return high, (x - high.astype(F32)).astype(BF)


def dot2(a, b, dims=((1,), (0,))):
    high, low = split(a)
    return dotf(high, b, dims) + dotf(low, b, dims)


def inverses(lowers, ii, jj):
    diff = lax.bitwise_xor(ii, jj)
    eye = (ii == jj).astype(F32)
    low_b = [m.astype(BF) for m in lowers]
    zero = jnp.zeros((), BF)
    inv = [eye - jnp.where(diff == 1, m, 0.0) for m in lowers]
    for b in (2, 4, 8):
        mask = (diff >= b) & (diff < 2 * b)
        cross = [jnp.where(mask, m, zero) for m in low_b]
        inv_b = [x.astype(BF) for x in inv]
        ys = [dotf(c, x).astype(BF) for c, x in zip(cross, inv_b)]
        zs = [dotf(x, y) for x, y in zip(inv_b, ys)]
        inv = [x - z for x, z in zip(inv, zs)]
    for b in (16, 32, 64):
        mask = (diff >= b) & (diff < 2 * b)

        def lower_rows(a):
            return jnp.concatenate([a[o + b : o + 2 * b] for o in range(0, C, 2 * b)], 0)

        mask_low = lower_rows(mask)
        cross = [jnp.where(mask_low, lower_rows(m), zero) for m in low_b]
        inv_b = [x.astype(BF) for x in inv]
        ys = [dotf(c, x).astype(BF) for c, x in zip(cross, inv_b)]
        pad = jnp.zeros((b, C), BF)
        full = []
        for y in ys:
            parts = []
            for k in range(C // (2 * b)):
                parts += [pad, y[k * b : (k + 1) * b]]
            full.append(jnp.concatenate(parts, 0))
        zs = [dotf(lower_rows(x), y) for x, y in zip(inv_b, full)]
        out = []
        for x, z in zip(inv, zs):
            parts = []
            for k in range(C // (2 * b)):
                o = k * 2 * b
                parts += [x[o : o + b], x[o + b : o + 2 * b] - z[k * b : (k + 1) * b]]
            out.append(jnp.concatenate(parts, 0))
        inv = out
    inv_b = [x.astype(BF) for x in inv]
    prods = [dot2(m, x) for m, x in zip(lowers, inv_b)]
    errs = [(eye - x.astype(F32) - p).astype(BF) for x, p in zip(inv_b, prods)]
    return [x.astype(F32) + dotf(x, e) for x, e in zip(inv_b, errs)]


def setup_gates(decay, rate, g_ref, gt_ref, bt_ref):
    ii = lax.broadcasted_iota(jnp.int32, (C, C), 0)
    jj = lax.broadcasted_iota(jnp.int32, (C, C), 1)
    tri = (ii >= jj).astype(F32)
    for c in range(NCH):
        sl = slice(c * C, (c + 1) * C)
        g_ref[sl, :] = jnp.dot(tri, decay[sl, :], precision=lax.Precision.HIGHEST, preferred_element_type=F32)
    gt_ref[...] = g_ref[...].T
    bt_ref[...] = rate.T


def local_heads(heads, q, k, v, g_all, b_all, gt_ref, bt_ref):
    ii = lax.broadcasted_iota(jnp.int32, (C, C), 0)
    jj = lax.broadcasted_iota(jnp.int32, (C, C), 1)
    tri = ii >= jj
    strict = ii > jj
    eye = (ii == jj).astype(F32)
    lane = lax.broadcasted_iota(jnp.int32, g_all.shape, 1)
    kns, qs, vs, gcs, grs, brs, bcs = [], [], [], [], [], [], []
    for n, h in enumerate(heads):
        kf = k[n].astype(F32)
        kn = (kf * lax.rsqrt(jnp.sum(kf * kf, axis=-1, keepdims=True) + 1e-6)).astype(BF)
        gcol = jnp.sum(jnp.where(lane == h, g_all, 0.0), axis=1, keepdims=True)
        bcol = jnp.sum(jnp.where(lane == h, b_all, 0.0), axis=1, keepdims=True)
        grow = gt_ref[pl.ds(h, 1), :]
        brow = bt_ref[pl.ds(h, 1), :]
        for c in range(NCH):
            sl = slice(c * C, (c + 1) * C)
            kns.append(kn[sl])
            qs.append(q[n][sl])
            vs.append(v[n][sl])
            gcs.append(gcol[sl])
            bcs.append(bcol[sl])
            grs.append(grow[:, sl])
            brs.append(brow[:, sl])
    falls = [jnp.exp(jnp.where(tri, gc - gr, -1e30)) for gc, gr in zip(gcs, grs)]
    gram = [dotf(a, a, NT) for a in kns]
    qk = [dotf(a, b, NT) for a, b in zip(qs, kns)]
    lowers = [jnp.where(strict, bc * d * g, 0.0) for bc, d, g in zip(bcs, falls, gram)]
    scores = [(a * d).astype(BF) for a, d in zip(qk, falls)]
    inv = inverses(lowers, ii, jj)
    egr = [jnp.exp(g) for g in grs]
    egc = [jnp.exp(g) for g in gcs]
    wv = [dot2(x * b, vv) for x, b, vv in zip(inv, brs, vs)]
    wk = [dot2(x * (b * e), kk) for x, b, e, kk in zip(inv, brs, egr, kns)]
    count = len(heads)
    near, rows = [[] for _ in heads], [[] for _ in heads]
    pair = [None] * count
    for c in range(NCH):
        for n in range(count):
            i = n * NCH + c
            glast = gcs[i][C - 1 : C, :]
            fall = jnp.exp(glast)
            tail = jnp.exp(glast - gcs[i])
            if c == 0:
                errors = jnp.concatenate([wv[i], -wk[i]], axis=1)
            else:
                pair_b = pair[n].astype(BF)
                errors = jnp.concatenate([wv[i], jnp.zeros_like(wv[i])], axis=1) - dotf(wk[i].astype(BF), pair_b)
            mixed = dotf(scores[i], errors.astype(BF))
            if c == 0:
                near_c = mixed[:, :128]
                rows_c = egc[i] * qs[i].astype(F32) + mixed[:, 128:]
            else:
                mixed = mixed + egc[i] * dotf(qs[i], pair_b)
                near_c = mixed[:, :128]
                rows_c = mixed[:, 128:]
            near[n].append(near_c)
            rows[n].append(rows_c.astype(BF))
            high, low = split(tail * errors)
            grown = dotf(kns[i], high, TN) + dotf(kns[i], low, TN)
            if c == 0:
                pair[n] = jnp.concatenate([jnp.zeros((128, 128), F32), fall * eye], axis=1) + grown
            else:
                pair[n] = fall * pair[n] + grown
    near = [jnp.concatenate(x, 0) for x in near]
    rows = [jnp.concatenate(x, 0) for x in rows]
    return near, rows, pair


def local_kernel(q_ref, k_ref, v_ref, ld_ref, b_ref, near_ref, rows_ref, run_ref, g_ref, gt_ref, bt_ref):
    p = pl.program_id(0)

    @pl.when(p == 0)
    def _():
        setup_gates(ld_ref[...], b_ref[...], g_ref, gt_ref, bt_ref)

    heads = [p * HP + n for n in range(HP)]

    def cut(ref):
        return [ref[:, n * 128 : (n + 1) * 128] for n in range(HP)]

    near, rows, pair = local_heads(
        heads, cut(q_ref), cut(k_ref), cut(v_ref), g_ref[...], b_ref[...], gt_ref, bt_ref
    )
    for n in range(HP):
        near_ref[:, n * 128 : (n + 1) * 128] = near[n]
        rows_ref[:, n * 128 : (n + 1) * 128] = rows[n]
        run_ref[n] = pair[n]


def local_call(q, k, v, decay, rate):
    wide = pl.BlockSpec((512, HP * 128), lambda p: (0, p))
    gate = pl.BlockSpec((512, 8), lambda p: (0, 0))
    run = pl.BlockSpec((HP, 128, 256), lambda p: (p, 0, 0))
    return pl.pallas_call(
        local_kernel,
        grid=(8 // HP,),
        in_specs=[wide, wide, wide, gate, gate],
        out_specs=[wide, wide, run],
        out_shape=[
            jax.ShapeDtypeStruct((512, 1024), F32),
            jax.ShapeDtypeStruct((512, 1024), BF),
            jax.ShapeDtypeStruct((8, 128, 256), F32),
        ],
        scratch_shapes=[pltpu.VMEM((512, 8), F32), pltpu.VMEM((8, 512), F32), pltpu.VMEM((8, 512), F32)],
        compiler_params=pltpu.CompilerParams(vmem_limit_bytes=56 << 20),
        name="local_pass",
    )(q, k, v, decay, rate)


def partner(array, axis, bit):
    return lax.ppermute(array, axis, [(i, i ^ 1 << bit) for i in range(lax.axis_size(axis))])


def low_product(form, left_op, right_op):
    return jnp.einsum(form, left_op, right_op, preferred_element_type=F32)


def finish(near, rows, carried, weights, levels_in):
    length, wide = near.shape
    head_count = wide // 128
    near_part = near.reshape(length, head_count, 128)
    row_part = rows.reshape(length, head_count, 128)
    far_part = low_product("thd,lhde->thle", row_part, carried.astype(BF))
    terms = jnp.concatenate([near_part[:, :, None], far_part], axis=2)
    level_ids = jnp.arange(LEVELS)
    keep_mask = (level_ids[None, :] < levels_in[:, None]).astype(weights.dtype)
    scaled = weights.reshape(length // BLOCK, BLOCK, head_count, LEVELS) * keep_mask[:, None, None, :]
    scaled = scaled.reshape(length, head_count, LEVELS)
    total = jnp.sum(scaled[..., None] * terms, axis=2)
    return total.astype(BF).reshape(length, wide)


def per_device(queries, key_rows, value_rows, log_decay, write_rate, level_weights, block_levels):
    near, rows, own = local_call(queries, key_rows, value_rows, log_decay, write_rate)
    bits_total = lax.axis_size("ctx").bit_length() - 1
    position = lax.axis_index("ctx")
    prefix = jnp.broadcast_to(jnp.eye(128, dtype=F32), (8, 128, 128))
    carried = []
    for section in range(bits_total):
        upper = position >> section & 1 == 1
        own_b = own.astype(BF)
        other_b = partner(own_b, "ctx", section)
        left = jnp.where(upper, other_b, own_b)
        both = jnp.matmul(prefix.astype(BF), other_b, preferred_element_type=F32)
        carried.append(jnp.where(upper, both[..., :128], 0.0))
        prefix = jnp.where(upper, both[..., 128:], prefix)
        if section + 1 < bits_total:
            right_trans = jnp.where(upper, own_b, other_b)[..., 128:]
            right_state = jnp.where(upper, own, other_b.astype(F32))[..., :128]
            joined = jnp.matmul(right_trans, left, preferred_element_type=F32)
            own = joined + jnp.concatenate([right_state, jnp.zeros_like(right_state)], axis=-1)
    outputs = finish(near, rows, jnp.stack(carried, axis=0), level_weights, block_levels)
    return lax.all_to_all(outputs, "head", split_axis=0, concat_axis=1, tiled=True)


def solution(mesh):
    in_specs = (P("ctx", "head"),) * 6 + (P("ctx"),)
    out_specs = P(("ctx", "head"), None)
    return jax.shard_map(per_device, mesh=mesh, in_specs=in_specs, out_specs=out_specs, check_vma=False)
```

```python
import jax
import jax.numpy as jnp
from jax import lax
from jax.experimental import pallas as pl
from jax.experimental.pallas import tpu as pltpu
from jax.sharding import PartitionSpec as P

BLOCK = 64
LEVELS = 5
F32, BF = jnp.float32, jnp.bfloat16
C = 128
NCH = 4
HP = 2
NT = ((1,), (1,))
TN = ((0,), (0,))


def dotf(a, b, dims=((1,), (0,))):
    return lax.dot_general(a, b, (dims, ((), ())), preferred_element_type=F32)


def split(x):
    high = x.astype(BF)
    return high, (x - high.astype(F32)).astype(BF)


def dot2(a, b, dims=((1,), (0,))):
    high, low = split(a)
    return dotf(high, b, dims) + dotf(low, b, dims)


def inverses(lowers, ii, jj):
    diff = lax.bitwise_xor(ii, jj)
    eye = (ii == jj).astype(F32)
    low_b = [m.astype(BF) for m in lowers]
    zero = jnp.zeros((), BF)
    inv = [eye - jnp.where(diff == 1, m, 0.0) for m in lowers]
    for b in (2, 4, 8):
        mask = (diff >= b) & (diff < 2 * b)
        cross = [jnp.where(mask, m, zero) for m in low_b]
        inv_b = [x.astype(BF) for x in inv]
        ys = [dotf(c, x).astype(BF) for c, x in zip(cross, inv_b)]
        zs = [dotf(x, y) for x, y in zip(inv_b, ys)]
        inv = [x - z for x, z in zip(inv, zs)]
    for b in (16, 32, 64):
        mask = (diff >= b) & (diff < 2 * b)

        def lower_rows(a):
            return jnp.concatenate([a[o + b : o + 2 * b] for o in range(0, C, 2 * b)], 0)

        mask_low = lower_rows(mask)
        cross = [jnp.where(mask_low, lower_rows(m), zero) for m in low_b]
        inv_b = [x.astype(BF) for x in inv]
        ys = [dotf(c, x).astype(BF) for c, x in zip(cross, inv_b)]
        pad = jnp.zeros((b, C), BF)
        full = []
        for y in ys:
            parts = []
            for k in range(C // (2 * b)):
                parts += [pad, y[k * b : (k + 1) * b]]
            full.append(jnp.concatenate(parts, 0))
        zs = [dotf(lower_rows(x), y) for x, y in zip(inv_b, full)]
        out = []
        for x, z in zip(inv, zs):
            parts = []
            for k in range(C // (2 * b)):
                o = k * 2 * b
                parts += [x[o : o + b], x[o + b : o + 2 * b] - z[k * b : (k + 1) * b]]
            out.append(jnp.concatenate(parts, 0))
        inv = out
    inv_b = [x.astype(BF) for x in inv]
    prods = [dot2(m, x) for m, x in zip(lowers, inv_b)]
    errs = [(eye - x.astype(F32) - p).astype(BF) for x, p in zip(inv_b, prods)]
    return [x.astype(F32) + dotf(x, e) for x, e in zip(inv_b, errs)]


def setup_gates(decay_t, rate_t, g_ref, b_ref, gt_ref):
    ii = lax.broadcasted_iota(jnp.int32, (C, C), 0)
    jj = lax.broadcasted_iota(jnp.int32, (C, C), 1)
    tri = (ii <= jj).astype(F32)
    for c in range(NCH):
        sl = slice(c * C, (c + 1) * C)
        gt_ref[:, sl] = jnp.dot(
            decay_t[:, sl], tri, precision=lax.Precision.HIGHEST, preferred_element_type=F32
        )
    g_ref[...] = gt_ref[...].T
    b_ref[...] = rate_t.T


def local_heads(heads, q, k, v, g_all, b_all, gt_ref, bt_ref):
    ii = lax.broadcasted_iota(jnp.int32, (C, C), 0)
    jj = lax.broadcasted_iota(jnp.int32, (C, C), 1)
    tri = ii >= jj
    strict = ii > jj
    eye = (ii == jj).astype(F32)
    lane = lax.broadcasted_iota(jnp.int32, g_all.shape, 1)
    kns, qs, vs, gcs, grs, brs, bcs = [], [], [], [], [], [], []
    for n, h in enumerate(heads):
        kf = k[n].astype(F32)
        kn = (kf * lax.rsqrt(jnp.sum(kf * kf, axis=-1, keepdims=True) + 1e-6)).astype(BF)
        gcol = jnp.sum(jnp.where(lane == h, g_all, 0.0), axis=1, keepdims=True)
        bcol = jnp.sum(jnp.where(lane == h, b_all, 0.0), axis=1, keepdims=True)
        grow = gt_ref[pl.ds(h, 1), :]
        brow = bt_ref[pl.ds(h, 1), :]
        for c in range(NCH):
            sl = slice(c * C, (c + 1) * C)
            kns.append(kn[sl])
            qs.append(q[n][sl])
            vs.append(v[n][sl])
            gcs.append(gcol[sl])
            bcs.append(bcol[sl])
            grs.append(grow[:, sl])
            brs.append(brow[:, sl])
    falls = [jnp.exp(jnp.where(tri, gc - gr, -1e30)) for gc, gr in zip(gcs, grs)]
    gram = [dotf(a, a, NT) for a in kns]
    qk = [dotf(a, b, NT) for a, b in zip(qs, kns)]
    lowers = [jnp.where(strict, bc * d * g, 0.0) for bc, d, g in zip(bcs, falls, gram)]
    scores = [(a * d).astype(BF) for a, d in zip(qk, falls)]
    inv = inverses(lowers, ii, jj)
    egr = [jnp.exp(g) for g in grs]
    egc = [jnp.exp(g) for g in gcs]
    wv = [dot2(x * b, vv) for x, b, vv in zip(inv, brs, vs)]
    wk = [dot2(x * (b * e), kk) for x, b, e, kk in zip(inv, brs, egr, kns)]
    count = len(heads)
    near, rows = [[] for _ in heads], [[] for _ in heads]
    pair = [None] * count
    for c in range(NCH):
        for n in range(count):
            i = n * NCH + c
            glast = gcs[i][C - 1 : C, :]
            fall = jnp.exp(glast)
            tail = jnp.exp(glast - gcs[i])
            if c == 0:
                errors = jnp.concatenate([wv[i], -wk[i]], axis=1)
            else:
                pair_b = pair[n].astype(BF)
                errors = jnp.concatenate([wv[i], jnp.zeros_like(wv[i])], axis=1) - dotf(wk[i].astype(BF), pair_b)
            mixed = dotf(scores[i], errors.astype(BF))
            if c == 0:
                near_c = mixed[:, :128]
                rows_c = egc[i] * qs[i].astype(F32) + mixed[:, 128:]
            else:
                mixed = mixed + egc[i] * dotf(qs[i], pair_b)
                near_c = mixed[:, :128]
                rows_c = mixed[:, 128:]
            near[n].append(near_c)
            rows[n].append(rows_c.astype(BF))
            high, low = split(tail * errors)
            grown = dotf(kns[i], high, TN) + dotf(kns[i], low, TN)
            if c == 0:
                pair[n] = jnp.concatenate([jnp.zeros((128, 128), F32), fall * eye], axis=1) + grown
            else:
                pair[n] = fall * pair[n] + grown
    near = [jnp.concatenate(x, 0) for x in near]
    rows = [jnp.concatenate(x, 0) for x in rows]
    return near, rows, pair


def local_kernel(q_ref, k_ref, v_ref, ldt_ref, bt_ref, near_ref, rows_ref, run_ref, g_ref, b_ref, gt_ref):
    p = pl.program_id(0)

    @pl.when(p == 0)
    def _():
        setup_gates(ldt_ref[...], bt_ref[...], g_ref, b_ref, gt_ref)

    heads = [p * HP + n for n in range(HP)]

    def cut(ref):
        return [ref[:, n * 128 : (n + 1) * 128] for n in range(HP)]

    near, rows, pair = local_heads(
        heads, cut(q_ref), cut(k_ref), cut(v_ref), g_ref[...], b_ref[...], gt_ref, bt_ref
    )
    for n in range(HP):
        near_ref[:, n * 128 : (n + 1) * 128] = near[n]
        rows_ref[:, n * 128 : (n + 1) * 128] = rows[n]
        run_ref[n] = pair[n]


def local_call(q, k, v, decay, rate):
    wide = pl.BlockSpec((512, HP * 128), lambda p: (0, p))
    gate = pl.BlockSpec((8, 512), lambda p: (0, 0))
    run = pl.BlockSpec((HP, 128, 256), lambda p: (p, 0, 0))
    return pl.pallas_call(
        local_kernel,
        grid=(8 // HP,),
        in_specs=[wide, wide, wide, gate, gate],
        out_specs=[wide, wide, run],
        out_shape=[
            jax.ShapeDtypeStruct((512, 1024), F32),
            jax.ShapeDtypeStruct((512, 1024), BF),
            jax.ShapeDtypeStruct((8, 128, 256), F32),
        ],
        scratch_shapes=[pltpu.VMEM((512, 8), F32), pltpu.VMEM((512, 8), F32), pltpu.VMEM((8, 512), F32)],
        compiler_params=pltpu.CompilerParams(vmem_limit_bytes=56 << 20),
        name="local_pass",
    )(q, k, v, decay.T, rate.T)


MESH = pl.DeviceIdType.MESH
HEADS = 8
LEV = 4


def exchange_kernel(
    near_ref, rows_ref, run_ref, wt_ref, lev_ref, out_ref,
    sent, got, sent_s, got_s, run_f, prefix, carried, w_ref, stage,
    send_sem, recv_sem, out_send, out_recv, own_sem,
):
    pos = lax.axis_index("ctx")
    me = lax.axis_index("head")
    bits = [(pos // 2**r) % 2 for r in range(LEV)]
    mates = [pos + (1 - 2 * bits[r]) * 2**r for r in range(LEV)]
    peers = [lax.rem(me + d, HEADS) for d in range(1, HEADS)]

    barrier = pltpu.get_barrier_semaphore()
    for m in mates:
        pl.semaphore_signal(barrier, inc=1, device_id={"ctx": m}, device_id_type=MESH)
    for j in peers:
        pl.semaphore_signal(barrier, inc=1, device_id={"head": j}, device_id_type=MESH)
    pl.semaphore_wait(barrier, LEV + HEADS - 1)

    def run_copy(r, h):
        if r == LEV - 1:
            src, dst = sent_s.at[h], got_s.at[h]
        else:
            src, dst = sent.at[r, h], got.at[r, h]
        return pltpu.make_async_remote_copy(
            src_ref=src,
            dst_ref=dst,
            send_sem=send_sem.at[r, h],
            recv_sem=recv_sem.at[r, h],
            device_id={"ctx": mates[r]},
            device_id_type=MESH,
        )

    def head_cols(h):
        return pl.ds(pl.multiple_of(h * 128, 128), 128)

    def out_copy(h, src_dev, dst_dev):
        cols = pl.ds(pl.multiple_of(src_dev * 1024 + h * 128, 128), 128)
        return pltpu.make_async_remote_copy(
            src_ref=stage.at[pl.ds(pl.multiple_of(dst_dev * 64, 64), 64), head_cols(h)],
            dst_ref=out_ref.at[:, cols],
            send_sem=out_send.at[h, dst_dev],
            recv_sem=out_recv.at[h, src_dev],
            device_id={"head": dst_dev},
            device_id_type=MESH,
        )

    def own_copy(h):
        cols = pl.ds(pl.multiple_of(me * 1024 + h * 128, 128), 128)
        return pltpu.make_async_copy(
            stage.at[pl.ds(pl.multiple_of(me * 64, 64), 64), head_cols(h)], out_ref.at[:, cols], own_sem.at[h]
        )

    @pl.loop(0, HEADS)
    def _(h):
        sent[0, h] = run_ref[h].astype(BF)
        run_copy(0, h).start()

    lane = lax.broadcasted_iota(jnp.int32, (64, 40), 1)
    level = lane
    for m in range(1, HEADS):
        level = jnp.where(lane >= LEVELS * m, lane - LEVELS * m, level)
    w_all = wt_ref[...].T
    for n in range(8):
        sl = slice(64 * n, 64 * n + 64)
        w_ref[sl, :] = jnp.where(level < lev_ref[n], w_all[sl], 0.0)

    lanes = lax.broadcasted_iota(jnp.int32, (512, 40), 1)

    def finish(h):
        w = w_ref[...]
        weight = [
            jnp.sum(jnp.where(lanes == h * LEVELS + i, w, 0.0), axis=1, keepdims=True) for i in range(LEVELS)
        ]
        far = dotf(rows_ref[:, head_cols(h)], carried[h])
        total = weight[0] * near_ref[:, head_cols(h)]
        for i in range(LEV):
            total = total + weight[i + 1] * far[:, i * 128 : (i + 1) * 128]
        stage[:, head_cols(h)] = total.astype(BF)
        for j in peers:
            out_copy(h, me, j).start()
        own_copy(h).start()

    for r in range(LEV):
        up = bits[r] == 1

        @pl.loop(0, HEADS)
        def _(h):
            run_copy(r, h).wait_recv()
            cr = slice(r * 128, (r + 1) * 128)
            if r == LEV - 1:
                other = got_s[h]
                far = dotf(prefix[h].astype(BF), other)
                carried[h, :, cr] = jnp.where(up, far, 0.0).astype(BF)
                finish(h)
                return
            other = got[r, h]
            own_b = sent[r, h]
            other_f = other.astype(F32)
            own_f = run_ref[h] if r == 0 else run_f[h]
            left = jnp.where(up, other_f, own_b.astype(F32)).astype(BF)
            right_t = jnp.where(up, own_b[:, 128:].astype(F32), other_f[:, 128:]).astype(BF)
            right_s = jnp.where(up, own_f[:, :128], other_f[:, :128])
            if r == 0:
                ii = lax.broadcasted_iota(jnp.int32, (128, 128), 0)
                jj = lax.broadcasted_iota(jnp.int32, (128, 128), 1)
                both = other_f
                old = (ii == jj).astype(F32)
            else:
                old = prefix[h]
                both = dotf(old.astype(BF), left)
            carried[h, :, cr] = jnp.where(up, both[:, :128], 0.0).astype(BF)
            prefix[h] = jnp.where(up, both[:, 128:], old)
            if r < LEV - 2:
                joined = dotf(right_t, left)
                joined = jnp.concatenate([joined[:, :128] + right_s, joined[:, 128:]], axis=1)
                run_f[h] = joined
                sent[r + 1, h] = joined.astype(BF)
            else:
                sent_s[h] = (dotf(right_t, left[:, :128]) + right_s).astype(BF)
            run_copy(r + 1, h).start()

    @pl.loop(0, HEADS)
    def _(h):
        for r in range(LEV):
            run_copy(r, h).wait_send()
        own_copy(h).wait()
        for j in peers:
            out_copy(h, me, j).wait_send()
        for j in peers:
            out_copy(h, j, me).wait_recv()


def exchange_call(near, rows, run, weights, levels_in):
    vmem = pl.BlockSpec(memory_space=pltpu.VMEM)
    return pl.pallas_call(
        exchange_kernel,
        in_specs=[vmem, vmem, vmem, vmem, pl.BlockSpec(memory_space=pltpu.SMEM)],
        out_specs=pl.BlockSpec(memory_space=pl.ANY),
        out_shape=jax.ShapeDtypeStruct((64, 8192), BF),
        scratch_shapes=[
            pltpu.VMEM((LEV - 1, HEADS, 128, 256), BF),
            pltpu.VMEM((LEV - 1, HEADS, 128, 256), BF),
            pltpu.VMEM((HEADS, 128, 128), BF),
            pltpu.VMEM((HEADS, 128, 128), BF),
            pltpu.VMEM((HEADS, 128, 256), F32),
            pltpu.VMEM((HEADS, 128, 128), F32),
            pltpu.VMEM((HEADS, 128, LEV * 128), BF),
            pltpu.VMEM((512, 40), F32),
            pltpu.VMEM((512, 1024), BF),
            pltpu.SemaphoreType.DMA((LEV, HEADS)),
            pltpu.SemaphoreType.DMA((LEV, HEADS)),
            pltpu.SemaphoreType.DMA((HEADS, HEADS)),
            pltpu.SemaphoreType.DMA((HEADS, HEADS)),
            pltpu.SemaphoreType.DMA((HEADS,)),
        ],
        compiler_params=pltpu.CompilerParams(
            collective_id=0, has_side_effects=True, vmem_limit_bytes=56 << 20
        ),
        name="exchange",
    )(near, rows, run, weights.T, levels_in)


def per_device(queries, key_rows, value_rows, log_decay, write_rate, level_weights, block_levels):
    near, rows, run = local_call(queries, key_rows, value_rows, log_decay, write_rate)
    return exchange_call(near, rows, run, level_weights, block_levels)


def solution(mesh):
    in_specs = (P("ctx", "head"),) * 6 + (P("ctx"),)
    out_specs = P(("ctx", "head"), None)
    return jax.shard_map(per_device, mesh=mesh, in_specs=in_specs, out_specs=out_specs, check_vma=False)
```

```python
import jax
import jax.numpy as jnp
from jax import lax
from jax.experimental import pallas as pl
from jax.experimental.pallas import tpu as pltpu
from jax.sharding import PartitionSpec as P

BLOCK = 64
LEVELS = 5
F32, BF = jnp.float32, jnp.bfloat16
C = 128
NCH = 4
HP = 2
NT = ((1,), (1,))
TN = ((0,), (0,))


def dotf(a, b, dims=((1,), (0,))):
    return lax.dot_general(a, b, (dims, ((), ())), preferred_element_type=F32)


def split(x):
    high = x.astype(BF)
    return high, (x - high.astype(F32)).astype(BF)


def dot2(a, b, dims=((1,), (0,))):
    high, low = split(a)
    return dotf(high, b, dims) + dotf(low, b, dims)


def inverses(lowers, ii, jj):
    diff = lax.bitwise_xor(ii, jj)
    eye = (ii == jj).astype(F32)
    low_b = [m.astype(BF) for m in lowers]
    zero = jnp.zeros((), BF)
    inv = [eye - jnp.where(diff == 1, m, 0.0) for m in lowers]
    for b in (2, 4, 8):
        mask = (diff >= b) & (diff < 2 * b)
        cross = [jnp.where(mask, m, zero) for m in low_b]
        inv_b = [x.astype(BF) for x in inv]
        ys = [dotf(c, x).astype(BF) for c, x in zip(cross, inv_b)]
        zs = [dotf(x, y) for x, y in zip(inv_b, ys)]
        inv = [x - z for x, z in zip(inv, zs)]
    for b in (16, 32, 64):
        mask = (diff >= b) & (diff < 2 * b)

        def lower_rows(a):
            return jnp.concatenate([a[o + b : o + 2 * b] for o in range(0, C, 2 * b)], 0)

        mask_low = lower_rows(mask)
        cross = [jnp.where(mask_low, lower_rows(m), zero) for m in low_b]
        inv_b = [x.astype(BF) for x in inv]
        ys = [dotf(c, x).astype(BF) for c, x in zip(cross, inv_b)]
        pad = jnp.zeros((b, C), BF)
        full = []
        for y in ys:
            parts = []
            for k in range(C // (2 * b)):
                parts += [pad, y[k * b : (k + 1) * b]]
            full.append(jnp.concatenate(parts, 0))
        zs = [dotf(lower_rows(x), y) for x, y in zip(inv_b, full)]
        out = []
        for x, z in zip(inv, zs):
            parts = []
            for k in range(C // (2 * b)):
                o = k * 2 * b
                parts += [x[o : o + b], x[o + b : o + 2 * b] - z[k * b : (k + 1) * b]]
            out.append(jnp.concatenate(parts, 0))
        inv = out
    inv_b = [x.astype(BF) for x in inv]
    prods = [dot2(m, x) for m, x in zip(lowers, inv_b)]
    errs = [(eye - x.astype(F32) - p).astype(BF) for x, p in zip(inv_b, prods)]
    return [x.astype(F32) + dotf(x, e) for x, e in zip(inv_b, errs)]


def setup_gates(decay_t, rate_t, g_ref, b_ref, gt_ref):
    ii = lax.broadcasted_iota(jnp.int32, (C, C), 0)
    jj = lax.broadcasted_iota(jnp.int32, (C, C), 1)
    tri = (ii <= jj).astype(F32)
    for c in range(NCH):
        sl = slice(c * C, (c + 1) * C)
        gt_ref[:, sl] = jnp.dot(
            decay_t[:, sl], tri, precision=lax.Precision.HIGHEST, preferred_element_type=F32
        )
    g_ref[...] = gt_ref[...].T
    b_ref[...] = rate_t.T


def local_heads(heads, q, k, v, g_all, b_all, gt_ref, bt_ref):
    ii = lax.broadcasted_iota(jnp.int32, (C, C), 0)
    jj = lax.broadcasted_iota(jnp.int32, (C, C), 1)
    tri = ii >= jj
    strict = ii > jj
    eye = (ii == jj).astype(F32)
    lane = lax.broadcasted_iota(jnp.int32, g_all.shape, 1)
    kns, qs, vs, gcs, grs, brs, bcs = [], [], [], [], [], [], []
    for n, h in enumerate(heads):
        kf = k[n].astype(F32)
        kn = (kf * lax.rsqrt(jnp.sum(kf * kf, axis=-1, keepdims=True) + 1e-6)).astype(BF)
        gcol = jnp.sum(jnp.where(lane == h, g_all, 0.0), axis=1, keepdims=True)
        bcol = jnp.sum(jnp.where(lane == h, b_all, 0.0), axis=1, keepdims=True)
        grow = gt_ref[pl.ds(h, 1), :]
        brow = bt_ref[pl.ds(h, 1), :]
        for c in range(NCH):
            sl = slice(c * C, (c + 1) * C)
            kns.append(kn[sl])
            qs.append(q[n][sl])
            vs.append(v[n][sl])
            gcs.append(gcol[sl])
            bcs.append(bcol[sl])
            grs.append(grow[:, sl])
            brs.append(brow[:, sl])
    falls = [jnp.exp(jnp.where(tri, gc - gr, -1e30)) for gc, gr in zip(gcs, grs)]
    gram = [dotf(a, a, NT) for a in kns]
    qk = [dotf(a, b, NT) for a, b in zip(qs, kns)]
    lowers = [jnp.where(strict, bc * d * g, 0.0) for bc, d, g in zip(bcs, falls, gram)]
    scores = [(a * d).astype(BF) for a, d in zip(qk, falls)]
    inv = inverses(lowers, ii, jj)
    egr = [jnp.exp(g) for g in grs]
    egc = [jnp.exp(g) for g in gcs]
    wv = [dot2(x * b, vv) for x, b, vv in zip(inv, brs, vs)]
    wk = [dot2(x * (b * e), kk) for x, b, e, kk in zip(inv, brs, egr, kns)]
    count = len(heads)
    near, rows = [[] for _ in heads], [[] for _ in heads]
    pair = [None] * count
    for c in range(NCH):
        for n in range(count):
            i = n * NCH + c
            glast = gcs[i][C - 1 : C, :]
            fall = jnp.exp(glast)
            tail = jnp.exp(glast - gcs[i])
            if c == 0:
                errors = jnp.concatenate([wv[i], -wk[i]], axis=1)
            else:
                pair_b = pair[n].astype(BF)
                errors = jnp.concatenate([wv[i], jnp.zeros_like(wv[i])], axis=1) - dotf(wk[i].astype(BF), pair_b)
            mixed = dotf(scores[i], errors.astype(BF))
            if c == 0:
                near_c = mixed[:, :128]
                rows_c = egc[i] * qs[i].astype(F32) + mixed[:, 128:]
            else:
                mixed = mixed + egc[i] * dotf(qs[i], pair_b)
                near_c = mixed[:, :128]
                rows_c = mixed[:, 128:]
            near[n].append(near_c)
            rows[n].append(rows_c.astype(BF))
            high, low = split(tail * errors)
            grown = dotf(kns[i], high, TN) + dotf(kns[i], low, TN)
            if c == 0:
                pair[n] = jnp.concatenate([jnp.zeros((128, 128), F32), fall * eye], axis=1) + grown
            else:
                pair[n] = fall * pair[n] + grown
    near = [jnp.concatenate(x, 0) for x in near]
    rows = [jnp.concatenate(x, 0) for x in rows]
    return near, rows, pair


MESH = pl.DeviceIdType.MESH
HEADS = 8
LEV = 4


def fused_kernel(
    q_hbm, k_hbm, v_hbm, ldt_ref, bt_ref, wt_ref, lev_ref, out_ref,
    q_ref, k_ref, v_ref, g_ref, b_ref, gt_ref, near_ref, rows_ref,
    box, box_s, run_f, prefix, carried, w_ref, stage,
    in_sem, send_sem, recv_sem, out_send, out_recv, own_sem,
):
    pos = lax.axis_index("ctx")
    me = lax.axis_index("head")
    bits = [(pos // 2**r) % 2 for r in range(LEV)]
    mates = [pos + (1 - 2 * bits[r]) * 2**r for r in range(LEV)]
    peers = [lax.rem(me + d, HEADS) for d in range(1, HEADS)]

    barrier = pltpu.get_barrier_semaphore()
    for m in mates:
        pl.semaphore_signal(barrier, inc=1, device_id={"ctx": m}, device_id_type=MESH)
    for j in peers:
        pl.semaphore_signal(barrier, inc=1, device_id={"head": j}, device_id_type=MESH)

    def in_copies(p):
        cols = pl.ds(pl.multiple_of(p * HP * 128, HP * 128), HP * 128)
        return [
            pltpu.make_async_copy(src.at[:, cols], dst.at[:, cols], in_sem.at[i, p])
            for i, (src, dst) in enumerate(((k_hbm, k_ref), (q_hbm, q_ref), (v_hbm, v_ref)))
        ]

    for p in range(HEADS // HP):
        for c in in_copies(p):
            c.start()

    def run_copy(r, h):
        if r == LEV - 1:
            src, dst = box_s.at[h, 0], box_s.at[h, 1]
        else:
            src, dst = box.at[r, h, 0], box.at[r, h, 1]
        return pltpu.make_async_remote_copy(
            src_ref=src,
            dst_ref=dst,
            send_sem=send_sem.at[r, h],
            recv_sem=recv_sem.at[r, h],
            device_id={"ctx": mates[r]},
            device_id_type=MESH,
        )

    def head_cols(h):
        return pl.ds(pl.multiple_of(h * 128, 128), 128)

    def out_copy(h, src_dev, dst_dev):
        cols = pl.ds(pl.multiple_of(src_dev * 1024 + h * 128, 128), 128)
        return pltpu.make_async_remote_copy(
            src_ref=stage.at[pl.ds(pl.multiple_of(dst_dev * 64, 64), 64), head_cols(h)],
            dst_ref=out_ref.at[:, cols],
            send_sem=out_send.at[h, dst_dev],
            recv_sem=out_recv.at[h, src_dev],
            device_id={"head": dst_dev},
            device_id_type=MESH,
        )

    def own_copy(h):
        cols = pl.ds(pl.multiple_of(me * 1024 + h * 128, 128), 128)
        return pltpu.make_async_copy(
            stage.at[pl.ds(pl.multiple_of(me * 64, 64), 64), head_cols(h)], out_ref.at[:, cols], own_sem.at[h]
        )

    setup_gates(ldt_ref[...], bt_ref[...], g_ref, b_ref, gt_ref)

    lane = lax.broadcasted_iota(jnp.int32, (64, 40), 1)
    level = lane
    for m in range(1, HEADS):
        level = jnp.where(lane >= LEVELS * m, lane - LEVELS * m, level)
    w_all = wt_ref[...].T
    for n in range(8):
        sl = slice(64 * n, 64 * n + 64)
        w_ref[sl, :] = jnp.where(level < lev_ref[n], w_all[sl], 0.0)

    lanes = lax.broadcasted_iota(jnp.int32, (512, 40), 1)

    def finish(h):
        w = w_ref[...]
        weight = [
            jnp.sum(jnp.where(lanes == h * LEVELS + i, w, 0.0), axis=1, keepdims=True) for i in range(LEVELS)
        ]
        far = dotf(rows_ref[:, head_cols(h)], carried[h])
        total = weight[0] * near_ref[:, head_cols(h)]
        for i in range(LEV):
            total = total + weight[i + 1] * far[:, i * 128 : (i + 1) * 128]
        stage[:, head_cols(h)] = total.astype(BF)
        for j in peers:
            out_copy(h, me, j).start()
        own_copy(h).start()

    def step(r, h):
        up = bits[r] == 1
        run_copy(r, h).wait_recv()
        cr = slice(r * 128, (r + 1) * 128)
        if r == LEV - 1:
            far = dotf(prefix[h].astype(BF), box_s[h, 1])
            carried[h, :, cr] = jnp.where(up, far, 0.0).astype(BF)
            finish(h)
            return
        left = box[r, h, bits[r]]
        right = box[r, h, 1 - bits[r]]
        right_s = jnp.where(up, run_f[h, :, :128], right[:, :128].astype(F32))
        if r == 0:
            ii = lax.broadcasted_iota(jnp.int32, (128, 128), 0)
            jj = lax.broadcasted_iota(jnp.int32, (128, 128), 1)
            both = left.astype(F32)
            old = (ii == jj).astype(F32)
        else:
            old = prefix[h]
            both = dotf(old.astype(BF), left)
        carried[h, :, cr] = jnp.where(up, both[:, :128], 0.0).astype(BF)
        prefix[h] = jnp.where(up, both[:, 128:], old)
        if r < LEV - 2:
            joined = dotf(right[:, 128:], left)
            state = joined[:, :128] + right_s
            run_f[h] = state
            box[r + 1, h, 0, :, :128] = state.astype(BF)
            box[r + 1, h, 0, :, 128:] = joined[:, 128:].astype(BF)
        else:
            box_s[h, 0] = (dotf(right[:, 128:], left[:, :128]) + right_s).astype(BF)
        run_copy(r + 1, h).start()

    def steps(r, lo, hi):
        @pl.loop(lo, hi)
        def _(h):
            step(r, h)

    pairs = HEADS // HP

    @pl.loop(0, pairs)
    def _(p):
        for c in in_copies(p):
            c.wait()
        heads = [p * HP + n for n in range(HP)]

        def cut(ref):
            return [ref[:, head_cols(h)] for h in heads]

        near, rows, pair = local_heads(heads, cut(q_ref), cut(k_ref), cut(v_ref), g_ref[...], b_ref[...], gt_ref, bt_ref)

        @pl.when(p == 0)
        def _():
            pl.semaphore_wait(barrier, LEV + HEADS - 1)

        for n, h in enumerate(heads):
            run_f[h] = pair[n][:, :128]
            box[0, h, 0] = pair[n].astype(BF)
            run_copy(0, h).start()
        for n, h in enumerate(heads):
            near_ref[:, head_cols(h)] = near[n]
            rows_ref[:, head_cols(h)] = rows[n]
        for r in range(LEV - 1):
            steps(r, HP * jnp.maximum(p - 1 - r, 0), HP * jnp.maximum(p - r, 0))

    for r, p in ((1, 2), (2, 1), (0, 3), (3, 0), (2, 2), (1, 3), (3, 1), (2, 3), (3, 2), (3, 3)):
        steps(r, HP * p, HP * p + HP)

    @pl.loop(0, HEADS)
    def _(h):
        for r in range(LEV):
            run_copy(r, h).wait_send()
        own_copy(h).wait()
        for j in peers:
            out_copy(h, me, j).wait_send()
        for j in peers:
            out_copy(h, j, me).wait_recv()


def fused_call(q, k, v, decay, rate, weights, levels_in):
    vmem = pl.BlockSpec(memory_space=pltpu.VMEM)
    hbm = pl.BlockSpec(memory_space=pl.ANY)
    return pl.pallas_call(
        fused_kernel,
        in_specs=[hbm, hbm, hbm, vmem, vmem, vmem, pl.BlockSpec(memory_space=pltpu.SMEM)],
        out_specs=hbm,
        out_shape=jax.ShapeDtypeStruct((64, 8192), BF),
        scratch_shapes=[
            pltpu.VMEM((512, 1024), BF),
            pltpu.VMEM((512, 1024), BF),
            pltpu.VMEM((512, 1024), BF),
            pltpu.VMEM((512, 8), F32),
            pltpu.VMEM((512, 8), F32),
            pltpu.VMEM((8, 512), F32),
            pltpu.VMEM((512, 1024), F32),
            pltpu.VMEM((512, 1024), BF),
            pltpu.VMEM((LEV - 1, HEADS, 2, 128, 256), BF),
            pltpu.VMEM((HEADS, 2, 128, 128), BF),
            pltpu.VMEM((HEADS, 128, 128), F32),
            pltpu.VMEM((HEADS, 128, 128), F32),
            pltpu.VMEM((HEADS, 128, LEV * 128), BF),
            pltpu.VMEM((512, 40), F32),
            pltpu.VMEM((512, 1024), BF),
            pltpu.SemaphoreType.DMA((3, HEADS // HP)),
            pltpu.SemaphoreType.DMA((LEV, HEADS)),
            pltpu.SemaphoreType.DMA((LEV, HEADS)),
            pltpu.SemaphoreType.DMA((HEADS, HEADS)),
            pltpu.SemaphoreType.DMA((HEADS, HEADS)),
            pltpu.SemaphoreType.DMA((HEADS,)),
        ],
        compiler_params=pltpu.CompilerParams(
            collective_id=0, has_side_effects=True, vmem_limit_bytes=56 << 20
        ),
        name="fused",
    )(q, k, v, decay.T, rate.T, weights.T, levels_in)


def solution(mesh):
    in_specs = (P("ctx", "head"),) * 6 + (P("ctx"),)
    out_specs = P(("ctx", "head"), None)
    return jax.shard_map(fused_call, mesh=mesh, in_specs=in_specs, out_specs=out_specs, check_vma=False)
```

```python
import jax
import jax.numpy as jnp
from jax import lax
from jax.experimental import pallas as pl
from jax.experimental.pallas import tpu as pltpu
from jax.sharding import PartitionSpec as P

BLOCK = 64
LEVELS = 5
F32, BF = jnp.float32, jnp.bfloat16
C = 128
NCH = 4
HP = 4
NT = ((1,), (1,))
TN = ((0,), (0,))


def dotf(a, b, dims=((1,), (0,))):
    return lax.dot_general(a, b, (dims, ((), ())), preferred_element_type=F32)


def split(x):
    high = x.astype(BF)
    return high, (x - high.astype(F32)).astype(BF)


def dot2(a, b):
    return dotf(jnp.concatenate(split(a), 1), jnp.concatenate([b, b], 0))


def inverses(lowers, ii, jj):
    diff = lax.bitwise_xor(ii, jj)
    eye = (ii == jj).astype(F32)
    low_b = [m.astype(BF) for m in lowers]
    zero = jnp.zeros((), BF)
    inv = [eye - jnp.where(diff == 1, m, 0.0) for m in lowers]
    for b in (2, 4, 8):
        mask = (diff >= b) & (diff < 2 * b)
        cross = [jnp.where(mask, m, zero) for m in low_b]
        inv_b = [x.astype(BF) for x in inv]
        ys = [dotf(c, x).astype(BF) for c, x in zip(cross, inv_b)]
        zs = [dotf(x, y) for x, y in zip(inv_b, ys)]
        inv = [x - z for x, z in zip(inv, zs)]
    for b in (16, 32, 64):
        mask = (diff >= b) & (diff < 2 * b)

        def lower_rows(a):
            return jnp.concatenate([a[o + b : o + 2 * b] for o in range(0, C, 2 * b)], 0)

        mask_low = lower_rows(mask)
        cross = [jnp.where(mask_low, lower_rows(m), zero) for m in low_b]
        inv_b = [x.astype(BF) for x in inv]
        ys = [dotf(c, x).astype(BF) for c, x in zip(cross, inv_b)]
        pad = jnp.zeros((b, C), BF)
        full = []
        for y in ys:
            parts = []
            for k in range(C // (2 * b)):
                parts += [pad, y[k * b : (k + 1) * b]]
            full.append(jnp.concatenate(parts, 0))
        zs = [dotf(lower_rows(x), y) for x, y in zip(inv_b, full)]
        out = []
        for x, z in zip(inv, zs):
            parts = []
            for k in range(C // (2 * b)):
                o = k * 2 * b
                parts += [x[o : o + b], x[o + b : o + 2 * b] - z[k * b : (k + 1) * b]]
            out.append(jnp.concatenate(parts, 0))
        inv = out
    inv_b = [x.astype(BF) for x in inv]
    prods = [dot2(m, x) for m, x in zip(lowers, inv_b)]
    errs = [(eye - x.astype(F32) - p).astype(BF) for x, p in zip(inv_b, prods)]
    return [x.astype(F32) + dotf(x, e) for x, e in zip(inv_b, errs)]


def setup_gates(decay_t, rate_t, g_ref, b_ref, gt_ref):
    ii = lax.broadcasted_iota(jnp.int32, (C, C), 0)
    jj = lax.broadcasted_iota(jnp.int32, (C, C), 1)
    tri = (ii <= jj).astype(F32)
    for c in range(NCH):
        sl = slice(c * C, (c + 1) * C)
        gt_ref[:, sl] = jnp.dot(
            decay_t[:, sl], tri, precision=lax.Precision.HIGHEST, preferred_element_type=F32
        )
    g_ref[...] = gt_ref[...].T
    b_ref[...] = rate_t.T


def local_heads(heads, q, k, v, g_all, b_all, gt_ref, bt_ref):
    ii = lax.broadcasted_iota(jnp.int32, (C, C), 0)
    jj = lax.broadcasted_iota(jnp.int32, (C, C), 1)
    tri = ii >= jj
    strict = ii > jj
    eye = (ii == jj).astype(F32)
    lane = lax.broadcasted_iota(jnp.int32, g_all.shape, 1)
    kns, qs, vs, gcs, grs, brs, bcs = [], [], [], [], [], [], []
    for n, h in enumerate(heads):
        kf = k[n].astype(F32)
        kn = (kf * lax.rsqrt(jnp.sum(kf * kf, axis=-1, keepdims=True) + 1e-6)).astype(BF)
        gcol = jnp.sum(jnp.where(lane == h, g_all, 0.0), axis=1, keepdims=True)
        bcol = jnp.sum(jnp.where(lane == h, b_all, 0.0), axis=1, keepdims=True)
        grow = gt_ref[pl.ds(h, 1), :]
        brow = bt_ref[pl.ds(h, 1), :]
        for c in range(NCH):
            sl = slice(c * C, (c + 1) * C)
            kns.append(kn[sl])
            qs.append(q[n][sl])
            vs.append(v[n][sl])
            gcs.append(gcol[sl])
            bcs.append(bcol[sl])
            grs.append(grow[:, sl])
            brs.append(brow[:, sl])
    falls = [jnp.exp(jnp.where(tri, gc - gr, -1e30)) for gc, gr in zip(gcs, grs)]
    gram = [dotf(a, a, NT) for a in kns]
    qk = [dotf(a, b, NT) for a, b in zip(qs, kns)]
    lowers = [jnp.where(strict, bc * d * g, 0.0) for bc, d, g in zip(bcs, falls, gram)]
    scores = [(a * d).astype(BF) for a, d in zip(qk, falls)]
    inv = inverses(lowers, ii, jj)
    egr = [jnp.exp(g) for g in grs]
    egc = [jnp.exp(g) for g in gcs]
    wv = [dot2(x * b, vv) for x, b, vv in zip(inv, brs, vs)]
    wk = [dot2(x * (b * e), kk) for x, b, e, kk in zip(inv, brs, egr, kns)]
    count = len(heads)
    near, rows = [[] for _ in heads], [[] for _ in heads]
    pair = [None] * count
    for c in range(NCH):
        for n in range(count):
            i = n * NCH + c
            glast = gcs[i][C - 1 : C, :]
            fall = jnp.exp(glast)
            tail = jnp.exp(glast - gcs[i])
            if c == 0:
                errors = jnp.concatenate([wv[i], -wk[i]], axis=1)
            else:
                pair_b = pair[n].astype(BF)
                errors = jnp.concatenate([wv[i], jnp.zeros_like(wv[i])], axis=1) - dotf(wk[i].astype(BF), pair_b)
            mixed = dotf(scores[i], errors.astype(BF))
            if c == 0:
                near_c = mixed[:, :128]
                rows_c = egc[i] * qs[i].astype(F32) + mixed[:, 128:]
            else:
                mixed = mixed + egc[i] * dotf(qs[i], pair_b)
                near_c = mixed[:, :128]
                rows_c = mixed[:, 128:]
            near[n].append(near_c)
            rows[n].append(rows_c.astype(BF))
            grown = dotf(jnp.concatenate([kns[i], kns[i]], 0), jnp.concatenate(split(tail * errors), 0), TN)
            if c == 0:
                pair[n] = jnp.concatenate([jnp.zeros((128, 128), F32), fall * eye], axis=1) + grown
            else:
                pair[n] = fall * pair[n] + grown
    near = [jnp.concatenate(x, 0) for x in near]
    rows = [jnp.concatenate(x, 0) for x in rows]
    return near, rows, pair


MESH = pl.DeviceIdType.MESH
HEADS = 8
LEV = 4


def fused_kernel(
    q_hbm, k_hbm, v_hbm, ldt_ref, bt_ref, wt_ref, lev_ref, out_ref,
    q_ref, k_ref, v_ref, g_ref, b_ref, gt_ref, near_ref, rows_ref,
    box, box_s, run_f, prefix, carried, w_ref, stage,
    in_sem, send_sem, recv_sem, out_send, out_recv, own_sem,
):
    pos = lax.axis_index("ctx")
    me = lax.axis_index("head")
    bits = [(pos // 2**r) % 2 for r in range(LEV)]
    x, z = pos // 4, pos % 4
    mates = [pos + 1 - 2 * bits[0], pos + 3 - 2 * z, pos + 4 - 8 * bits[2], pos + 12 - 8 * x]
    peers = [lax.rem(me + d, HEADS) for d in range(1, HEADS)]

    barrier = pltpu.get_barrier_semaphore()
    for m in mates:
        pl.semaphore_signal(barrier, inc=1, device_id={"ctx": m}, device_id_type=MESH)
    for j in peers:
        pl.semaphore_signal(barrier, inc=1, device_id={"head": j}, device_id_type=MESH)

    def in_copies(p):
        cols = pl.ds(pl.multiple_of(p * HP * 128, HP * 128), HP * 128)
        return [
            pltpu.make_async_copy(src.at[:, cols], dst.at[:, cols], in_sem.at[i, p])
            for i, (src, dst) in enumerate(((k_hbm, k_ref), (q_hbm, q_ref), (v_hbm, v_ref)))
        ]

    for p in range(HEADS // HP):
        for c in in_copies(p):
            c.start()

    def run_copy(r, h):
        if r == LEV - 1:
            src, dst = box_s.at[h, 0], box_s.at[h, 1]
        else:
            src, dst = box.at[r, h, 0], box.at[r, h, 1]
        return pltpu.make_async_remote_copy(
            src_ref=src,
            dst_ref=dst,
            send_sem=send_sem.at[r, h],
            recv_sem=recv_sem.at[r, h],
            device_id={"ctx": mates[r]},
            device_id_type=MESH,
        )

    def head_cols(h):
        return pl.ds(pl.multiple_of(h * 128, 128), 128)

    def out_copy(h, src_dev, dst_dev):
        cols = pl.ds(pl.multiple_of(src_dev * 1024 + h * 128, 128), 128)
        return pltpu.make_async_remote_copy(
            src_ref=stage.at[pl.ds(pl.multiple_of(dst_dev * 64, 64), 64), head_cols(h)],
            dst_ref=out_ref.at[:, cols],
            send_sem=out_send.at[h, dst_dev],
            recv_sem=out_recv.at[h, src_dev],
            device_id={"head": dst_dev},
            device_id_type=MESH,
        )

    def own_copy(h):
        cols = pl.ds(pl.multiple_of(me * 1024 + h * 128, 128), 128)
        return pltpu.make_async_copy(
            stage.at[pl.ds(pl.multiple_of(me * 64, 64), 64), head_cols(h)], out_ref.at[:, cols], own_sem.at[h]
        )

    setup_gates(ldt_ref[...], bt_ref[...], g_ref, b_ref, gt_ref)

    lane = lax.broadcasted_iota(jnp.int32, (64, 40), 1)
    level = lane
    for m in range(1, HEADS):
        level = jnp.where(lane >= LEVELS * m, lane - LEVELS * m, level)
    w_all = wt_ref[...].T
    for n in range(8):
        sl = slice(64 * n, 64 * n + 64)
        w_ref[sl, :] = jnp.where(level < lev_ref[n], w_all[sl], 0.0)

    lanes = lax.broadcasted_iota(jnp.int32, (512, 40), 1)

    def finish(h):
        w = w_ref[...]
        weight = [
            jnp.sum(jnp.where(lanes == h * LEVELS + i, w, 0.0), axis=1, keepdims=True) for i in range(LEVELS)
        ]
        far = dotf(rows_ref[:, head_cols(h)], carried[h])
        total = weight[0] * near_ref[:, head_cols(h)]
        for i in range(LEV):
            total = total + weight[i + 1] * far[:, i * 128 : (i + 1) * 128]
        stage[:, head_cols(h)] = total.astype(BF)
        for j in peers:
            out_copy(h, me, j).start()
        own_copy(h).start()

    def step(r, h):
        up = bits[r] == 1
        run_copy(r, h).wait_recv()
        cr = slice(r * 128, (r + 1) * 128)
        if r == LEV - 1:
            far = dotf(prefix[h].astype(BF), box_s[h, 1])
            carried[h, :, cr] = jnp.where(up, far, 0.0).astype(BF)
            finish(h)
            return
        left = box[r, h, bits[r]]
        right = box[r, h, 1 - bits[r]]
        right_s = jnp.where(up, run_f[h, :, :128], right[:, :128].astype(F32))
        if r == 0:
            ii = lax.broadcasted_iota(jnp.int32, (128, 128), 0)
            jj = lax.broadcasted_iota(jnp.int32, (128, 128), 1)
            both = left.astype(F32)
            old = (ii == jj).astype(F32)
        else:
            old = prefix[h]
            both = dotf(old.astype(BF), left)
        carried[h, :, cr] = jnp.where(up, both[:, :128], 0.0).astype(BF)
        prefix[h] = jnp.where(up, both[:, 128:], old)
        if r < LEV - 2:
            joined = dotf(right[:, 128:], left)
            state = joined[:, :128] + right_s
            run_f[h] = state
            box[r + 1, h, 0, :, :128] = state.astype(BF)
            box[r + 1, h, 0, :, 128:] = joined[:, 128:].astype(BF)
        else:
            box_s[h, 0] = (dotf(right[:, 128:], left[:, :128]) + right_s).astype(BF)
        run_copy(r + 1, h).start()

    pairs = HEADS // HP

    @pl.loop(0, pairs)
    def _(p):
        for c in in_copies(p):
            c.wait()
        heads = [p * HP + n for n in range(HP)]

        def cut(ref):
            return [ref[:, head_cols(h)] for h in heads]

        near, rows, pair = local_heads(heads, cut(q_ref), cut(k_ref), cut(v_ref), g_ref[...], b_ref[...], gt_ref, bt_ref)

        @pl.when(p == 0)
        def _():
            pl.semaphore_wait(barrier, LEV + HEADS - 1)

        for n, h in enumerate(heads):
            run_f[h] = pair[n][:, :128]
            box[0, h, 0] = pair[n].astype(BF)
            run_copy(0, h).start()
        for n, h in enumerate(heads):
            near_ref[:, head_cols(h)] = near[n]
            rows_ref[:, head_cols(h)] = rows[n]

    @pl.loop(0, HP)
    def _(h):
        step(0, h)

    for r in range(LEV - 1):

        @pl.loop(0, HP)
        def _(h):
            step(r, h + HP)
            step(r + 1, h)

    @pl.loop(HP, HEADS)
    def _(h):
        step(LEV - 1, h)

    @pl.loop(0, HEADS)
    def _(h):
        for r in range(LEV):
            run_copy(r, h).wait_send()
        own_copy(h).wait()
        for j in peers:
            out_copy(h, me, j).wait_send()
        for j in peers:
            out_copy(h, j, me).wait_recv()


def fused_call(q, k, v, decay, rate, weights, levels_in):
    vmem = pl.BlockSpec(memory_space=pltpu.VMEM)
    hbm = pl.BlockSpec(memory_space=pl.ANY)
    return pl.pallas_call(
        fused_kernel,
        in_specs=[hbm, hbm, hbm, vmem, vmem, vmem, pl.BlockSpec(memory_space=pltpu.SMEM)],
        out_specs=hbm,
        out_shape=jax.ShapeDtypeStruct((64, 8192), BF),
        scratch_shapes=[
            pltpu.VMEM((512, 1024), BF),
            pltpu.VMEM((512, 1024), BF),
            pltpu.VMEM((512, 1024), BF),
            pltpu.VMEM((512, 8), F32),
            pltpu.VMEM((512, 8), F32),
            pltpu.VMEM((8, 512), F32),
            pltpu.VMEM((512, 1024), F32),
            pltpu.VMEM((512, 1024), BF),
            pltpu.VMEM((LEV - 1, HEADS, 2, 128, 256), BF),
            pltpu.VMEM((HEADS, 2, 128, 128), BF),
            pltpu.VMEM((HEADS, 128, 128), F32),
            pltpu.VMEM((HEADS, 128, 128), F32),
            pltpu.VMEM((HEADS, 128, LEV * 128), BF),
            pltpu.VMEM((512, 40), F32),
            pltpu.VMEM((512, 1024), BF),
            pltpu.SemaphoreType.DMA((3, HEADS // HP)),
            pltpu.SemaphoreType.DMA((LEV, HEADS)),
            pltpu.SemaphoreType.DMA((LEV, HEADS)),
            pltpu.SemaphoreType.DMA((HEADS, HEADS)),
            pltpu.SemaphoreType.DMA((HEADS, HEADS)),
            pltpu.SemaphoreType.DMA((HEADS,)),
        ],
        compiler_params=pltpu.CompilerParams(
            collective_id=0, has_side_effects=True, vmem_limit_bytes=56 << 20
        ),
        name="fused",
    )(q, k, v, decay.T, rate.T, weights.T, levels_in)


def solution(mesh):
    in_specs = (P("ctx", "head"),) * 6 + (P("ctx"),)
    out_specs = P(("ctx", "head"), None)
    return jax.shard_map(fused_call, mesh=mesh, in_specs=in_specs, out_specs=out_specs, check_vma=False)
```

```python
import jax
import jax.numpy as jnp
from jax import lax
from jax.experimental import pallas as pl
from jax.experimental.pallas import tpu as pltpu
from jax.sharding import PartitionSpec as P

BLOCK = 64
LEVELS = 5
F32, BF = jnp.float32, jnp.bfloat16
C = 128
NCH = 4
HP = 4
NT = ((1,), (1,))
TN = ((0,), (0,))


def dotf(a, b, dims=((1,), (0,))):
    return lax.dot_general(a, b, (dims, ((), ())), preferred_element_type=F32)


def split(x):
    high = x.astype(BF)
    return high, (x - high.astype(F32)).astype(BF)


def dot2(a, b):
    return dotf(jnp.concatenate(split(a), 1), jnp.concatenate([b, b], 0))


def inverses(lowers, ii, jj):
    diff = lax.bitwise_xor(ii, jj)
    eye = (ii == jj).astype(F32)
    low_b = [m.astype(BF) for m in lowers]
    zero = jnp.zeros((), BF)
    inv = [eye - jnp.where(diff == 1, m, 0.0) for m in lowers]
    for b in (2, 4, 8):
        mask = (diff >= b) & (diff < 2 * b)
        cross = [jnp.where(mask, m, zero) for m in low_b]
        inv_b = [x.astype(BF) for x in inv]
        ys = [dotf(c, x).astype(BF) for c, x in zip(cross, inv_b)]
        zs = [dotf(x, y) for x, y in zip(inv_b, ys)]
        inv = [x - z for x, z in zip(inv, zs)]
    for b in (16, 32, 64):
        mask = (diff >= b) & (diff < 2 * b)

        def lower_rows(a):
            return jnp.concatenate([a[o + b : o + 2 * b] for o in range(0, C, 2 * b)], 0)

        mask_low = lower_rows(mask)
        cross = [jnp.where(mask_low, lower_rows(m), zero) for m in low_b]
        inv_b = [x.astype(BF) for x in inv]
        ys = [dotf(c, x).astype(BF) for c, x in zip(cross, inv_b)]
        pad = jnp.zeros((b, C), BF)
        full = []
        for y in ys:
            parts = []
            for k in range(C // (2 * b)):
                parts += [pad, y[k * b : (k + 1) * b]]
            full.append(jnp.concatenate(parts, 0))
        zs = [dotf(lower_rows(x), y) for x, y in zip(inv_b, full)]
        out = []
        for x, z in zip(inv, zs):
            parts = []
            for k in range(C // (2 * b)):
                o = k * 2 * b
                parts += [x[o : o + b], x[o + b : o + 2 * b] - z[k * b : (k + 1) * b]]
            out.append(jnp.concatenate(parts, 0))
        inv = out
    inv_b = [x.astype(BF) for x in inv]
    prods = [dot2(m, x) for m, x in zip(lowers, inv_b)]
    errs = [(eye - x.astype(F32) - p).astype(BF) for x, p in zip(inv_b, prods)]
    return [x.astype(F32) + dotf(x, e) for x, e in zip(inv_b, errs)]


def setup_gates(decay_t, rate_t, g_ref, b_ref, gt_ref):
    ii = lax.broadcasted_iota(jnp.int32, (C, C), 0)
    jj = lax.broadcasted_iota(jnp.int32, (C, C), 1)
    tri = (ii <= jj).astype(F32)
    for c in range(NCH):
        sl = slice(c * C, (c + 1) * C)
        gt_ref[:, sl] = jnp.dot(
            decay_t[:, sl], tri, precision=lax.Precision.HIGHEST, preferred_element_type=F32
        )
    g_ref[...] = gt_ref[...].T
    b_ref[...] = rate_t.T


def local_heads(heads, q, k, v, g_all, b_all, gt_ref, bt_ref, between):
    ii = lax.broadcasted_iota(jnp.int32, (C, C), 0)
    jj = lax.broadcasted_iota(jnp.int32, (C, C), 1)
    tri = ii >= jj
    strict = ii > jj
    eye = (ii == jj).astype(F32)
    lane = lax.broadcasted_iota(jnp.int32, g_all.shape, 1)
    kns, qs, vs, gcs, grs, brs, bcs = [], [], [], [], [], [], []
    for n, h in enumerate(heads):
        kf = k[n].astype(F32)
        kn = (kf * lax.rsqrt(jnp.sum(kf * kf, axis=-1, keepdims=True) + 1e-6)).astype(BF)
        gcol = jnp.sum(jnp.where(lane == h, g_all, 0.0), axis=1, keepdims=True)
        bcol = jnp.sum(jnp.where(lane == h, b_all, 0.0), axis=1, keepdims=True)
        grow = gt_ref[pl.ds(h, 1), :]
        brow = bt_ref[pl.ds(h, 1), :]
        for c in range(NCH):
            sl = slice(c * C, (c + 1) * C)
            kns.append(kn[sl])
            qs.append(q[n][sl])
            vs.append(v[n][sl])
            gcs.append(gcol[sl])
            bcs.append(bcol[sl])
            grs.append(grow[:, sl])
            brs.append(brow[:, sl])
    falls = [jnp.exp(jnp.where(tri, gc - gr, -1e30)) for gc, gr in zip(gcs, grs)]
    gram = [dotf(a, a, NT) for a in kns]
    qk = [dotf(a, b, NT) for a, b in zip(qs, kns)]
    lowers = [jnp.where(strict, bc * d * g, 0.0) for bc, d, g in zip(bcs, falls, gram)]
    scores = [(a * d).astype(BF) for a, d in zip(qk, falls)]
    inv = inverses(lowers, ii, jj)
    between()
    egr = [jnp.exp(g) for g in grs]
    egc = [jnp.exp(g) for g in gcs]
    wv = [dot2(x * b, vv) for x, b, vv in zip(inv, brs, vs)]
    wk = [dot2(x * (b * e), kk) for x, b, e, kk in zip(inv, brs, egr, kns)]
    count = len(heads)
    near, rows = [[] for _ in heads], [[] for _ in heads]
    pair = [None] * count
    for c in range(NCH):
        for n in range(count):
            i = n * NCH + c
            glast = gcs[i][C - 1 : C, :]
            fall = jnp.exp(glast)
            tail = jnp.exp(glast - gcs[i])
            if c == 0:
                errors = jnp.concatenate([wv[i], -wk[i]], axis=1)
            else:
                pair_b = pair[n].astype(BF)
                errors = jnp.concatenate([wv[i], jnp.zeros_like(wv[i])], axis=1) - dotf(wk[i].astype(BF), pair_b)
            mixed = dotf(scores[i], errors.astype(BF))
            if c == 0:
                near_c = mixed[:, :128]
                rows_c = egc[i] * qs[i].astype(F32) + mixed[:, 128:]
            else:
                mixed = mixed + egc[i] * dotf(qs[i], pair_b)
                near_c = mixed[:, :128]
                rows_c = mixed[:, 128:]
            near[n].append(near_c)
            rows[n].append(rows_c.astype(BF))
            grown = dotf(jnp.concatenate([kns[i], kns[i]], 0), jnp.concatenate(split(tail * errors), 0), TN)
            if c == 0:
                pair[n] = jnp.concatenate([jnp.zeros((128, 128), F32), fall * eye], axis=1) + grown
            else:
                pair[n] = fall * pair[n] + grown
    near = [jnp.concatenate(x, 0) for x in near]
    rows = [jnp.concatenate(x, 0) for x in rows]
    return near, rows, pair


MESH = pl.DeviceIdType.MESH
HEADS = 8
LEV = 4
EARLY = 3


def fused_kernel(
    q_hbm, k_hbm, v_hbm, ldt_ref, bt_ref, wt_ref, lev_ref, out_ref,
    q_ref, k_ref, v_ref, g_ref, b_ref, gt_ref, near_ref, rows_ref,
    box, box_s, run_f, prefix, carried, w_ref, stage,
    in_sem, send_sem, recv_sem, out_send, out_recv, own_sem,
):
    pos = lax.axis_index("ctx")
    me = lax.axis_index("head")
    bits = [(pos // 2**r) % 2 for r in range(LEV)]
    x, z = pos // 4, pos % 4
    mates = [pos + 1 - 2 * bits[0], pos + 3 - 2 * z, pos + 4 - 8 * bits[2], pos + 12 - 8 * x]
    peers = [lax.rem(me + d, HEADS) for d in range(1, HEADS)]

    barrier = pltpu.get_barrier_semaphore()
    for m in mates:
        pl.semaphore_signal(barrier, inc=1, device_id={"ctx": m}, device_id_type=MESH)
    for j in peers:
        pl.semaphore_signal(barrier, inc=1, device_id={"head": j}, device_id_type=MESH)

    def in_copies(p):
        cols = pl.ds(pl.multiple_of(p * HP * 128, HP * 128), HP * 128)
        return [
            pltpu.make_async_copy(src.at[:, cols], dst.at[:, cols], in_sem.at[i, p])
            for i, (src, dst) in enumerate(((k_hbm, k_ref), (q_hbm, q_ref), (v_hbm, v_ref)))
        ]

    for p in range(HEADS // HP):
        for c in in_copies(p):
            c.start()

    def run_copy(r, h):
        if r == LEV - 1:
            src, dst = box_s.at[h, 0], box_s.at[h, 1]
        else:
            src, dst = box.at[r, h, 0], box.at[r, h, 1]
        return pltpu.make_async_remote_copy(
            src_ref=src,
            dst_ref=dst,
            send_sem=send_sem.at[r, h],
            recv_sem=recv_sem.at[r, h],
            device_id={"ctx": mates[r]},
            device_id_type=MESH,
        )

    def head_cols(h):
        return pl.ds(pl.multiple_of(h * 128, 128), 128)

    def out_copy(h, src_dev, dst_dev):
        cols = pl.ds(pl.multiple_of(src_dev * 1024 + h * 128, 128), 128)
        return pltpu.make_async_remote_copy(
            src_ref=stage.at[pl.ds(pl.multiple_of(dst_dev * 64, 64), 64), head_cols(h)],
            dst_ref=out_ref.at[:, cols],
            send_sem=out_send.at[h, dst_dev],
            recv_sem=out_recv.at[h, src_dev],
            device_id={"head": dst_dev},
            device_id_type=MESH,
        )

    def own_copy(h):
        cols = pl.ds(pl.multiple_of(me * 1024 + h * 128, 128), 128)
        return pltpu.make_async_copy(
            stage.at[pl.ds(pl.multiple_of(me * 64, 64), 64), head_cols(h)], out_ref.at[:, cols], own_sem.at[h]
        )

    setup_gates(ldt_ref[...], bt_ref[...], g_ref, b_ref, gt_ref)

    lane = lax.broadcasted_iota(jnp.int32, (64, 40), 1)
    level = lane
    for m in range(1, HEADS):
        level = jnp.where(lane >= LEVELS * m, lane - LEVELS * m, level)
    w_all = wt_ref[...].T
    for n in range(8):
        sl = slice(64 * n, 64 * n + 64)
        w_ref[sl, :] = jnp.where(level < lev_ref[n], w_all[sl], 0.0)

    lanes = lax.broadcasted_iota(jnp.int32, (512, 40), 1)

    def finish(h):
        w = w_ref[...]
        weight = [
            jnp.sum(jnp.where(lanes == h * LEVELS + i, w, 0.0), axis=1, keepdims=True) for i in range(LEVELS)
        ]
        far = dotf(rows_ref[:, head_cols(h)], carried[h])
        total = weight[0] * near_ref[:, head_cols(h)]
        for i in range(LEV):
            total = total + weight[i + 1] * far[:, i * 128 : (i + 1) * 128]
        stage[:, head_cols(h)] = total.astype(BF)
        for j in peers:
            out_copy(h, me, j).start()
        own_copy(h).start()

    def step(r, h):
        up = bits[r] == 1
        run_copy(r, h).wait_recv()
        cr = slice(r * 128, (r + 1) * 128)
        if r == LEV - 1:
            far = dotf(prefix[h].astype(BF), box_s[h, 1])
            carried[h, :, cr] = jnp.where(up, far, 0.0).astype(BF)
            finish(h)
            return
        left = box[r, h, bits[r]]
        right = box[r, h, 1 - bits[r]]
        right_s = jnp.where(up, run_f[h, :, :128], right[:, :128].astype(F32))
        if r == 0:
            ii = lax.broadcasted_iota(jnp.int32, (128, 128), 0)
            jj = lax.broadcasted_iota(jnp.int32, (128, 128), 1)
            both = left.astype(F32)
            old = (ii == jj).astype(F32)
        else:
            old = prefix[h]
            both = dotf(old.astype(BF), left)
        carried[h, :, cr] = jnp.where(up, both[:, :128], 0.0).astype(BF)
        prefix[h] = jnp.where(up, both[:, 128:], old)
        if r < LEV - 2:
            joined = dotf(right[:, 128:], left)
            state = joined[:, :128] + right_s
            run_f[h] = state
            box[r + 1, h, 0, :, :128] = state.astype(BF)
            box[r + 1, h, 0, :, 128:] = joined[:, 128:].astype(BF)
        else:
            box_s[h, 0] = (dotf(right[:, 128:], left[:, :128]) + right_s).astype(BF)
        run_copy(r + 1, h).start()

    pairs = HEADS // HP

    @pl.loop(0, pairs)
    def _(p):
        for c in in_copies(p):
            c.wait()
        heads = [p * HP + n for n in range(HP)]

        def cut(ref):
            return [ref[:, head_cols(h)] for h in heads]

        def between():
            @pl.when(p == 0)
            def _():
                pl.semaphore_wait(barrier, LEV + HEADS - 1)

            @pl.loop(0, EARLY * p)
            def _(h):
                step(0, h)

        near, rows, pair = local_heads(heads, cut(q_ref), cut(k_ref), cut(v_ref), g_ref[...], b_ref[...], gt_ref, bt_ref, between)

        for n, h in enumerate(heads):
            run_f[h] = pair[n][:, :128]
            box[0, h, 0] = pair[n].astype(BF)
            run_copy(0, h).start()
        for n, h in enumerate(heads):
            near_ref[:, head_cols(h)] = near[n]
            rows_ref[:, head_cols(h)] = rows[n]

    @pl.loop(EARLY, HP)
    def _(h):
        step(0, h)

    @pl.loop(0, HP)
    def _(h):
        step(1, h)

    for r in range(2):

        @pl.loop(0, HP)
        def _(h):
            step(r, h + HP)
            step(r + 2, h)

    @pl.loop(HP, HEADS)
    def _(h):
        step(LEV - 2, h)

    @pl.loop(HP, HEADS)
    def _(h):
        step(LEV - 1, h)

    @pl.loop(0, HEADS)
    def _(h):
        for r in range(LEV):
            run_copy(r, h).wait_send()
        own_copy(h).wait()
        for j in peers:
            out_copy(h, me, j).wait_send()
        for j in peers:
            out_copy(h, j, me).wait_recv()


def fused_call(q, k, v, decay, rate, weights, levels_in):
    vmem = pl.BlockSpec(memory_space=pltpu.VMEM)
    hbm = pl.BlockSpec(memory_space=pl.ANY)
    return pl.pallas_call(
        fused_kernel,
        in_specs=[hbm, hbm, hbm, vmem, vmem, vmem, pl.BlockSpec(memory_space=pltpu.SMEM)],
        out_specs=hbm,
        out_shape=jax.ShapeDtypeStruct((64, 8192), BF),
        scratch_shapes=[
            pltpu.VMEM((512, 1024), BF),
            pltpu.VMEM((512, 1024), BF),
            pltpu.VMEM((512, 1024), BF),
            pltpu.VMEM((512, 8), F32),
            pltpu.VMEM((512, 8), F32),
            pltpu.VMEM((8, 512), F32),
            pltpu.VMEM((512, 1024), F32),
            pltpu.VMEM((512, 1024), BF),
            pltpu.VMEM((LEV - 1, HEADS, 2, 128, 256), BF),
            pltpu.VMEM((HEADS, 2, 128, 128), BF),
            pltpu.VMEM((HEADS, 128, 128), F32),
            pltpu.VMEM((HEADS, 128, 128), F32),
            pltpu.VMEM((HEADS, 128, LEV * 128), BF),
            pltpu.VMEM((512, 40), F32),
            pltpu.VMEM((512, 1024), BF),
            pltpu.SemaphoreType.DMA((3, HEADS // HP)),
            pltpu.SemaphoreType.DMA((LEV, HEADS)),
            pltpu.SemaphoreType.DMA((LEV, HEADS)),
            pltpu.SemaphoreType.DMA((HEADS, HEADS)),
            pltpu.SemaphoreType.DMA((HEADS, HEADS)),
            pltpu.SemaphoreType.DMA((HEADS,)),
        ],
        compiler_params=pltpu.CompilerParams(
            collective_id=0, has_side_effects=True, vmem_limit_bytes=56 << 20
        ),
        name="fused",
    )(q, k, v, decay.T, rate.T, weights.T, levels_in)


def solution(mesh):
    in_specs = (P("ctx", "head"),) * 6 + (P("ctx"),)
    out_specs = P(("ctx", "head"), None)
    return jax.shard_map(fused_call, mesh=mesh, in_specs=in_specs, out_specs=out_specs, check_vma=False)
```

```python
import jax
import jax.numpy as jnp
from jax import lax
from jax.experimental import pallas as pl
from jax.experimental.pallas import tpu as pltpu
from jax.sharding import PartitionSpec as P

BLOCK = 64
LEVELS = 5
F32, BF = jnp.float32, jnp.bfloat16
C = 128
NCH = 4
NT = ((1,), (1,))
TN = ((0,), (0,))


def dotf(a, b, dims=((1,), (0,))):
    return lax.dot_general(a, b, (dims, ((), ())), preferred_element_type=F32)


def split(x):
    high = x.astype(BF)
    return high, (x - high.astype(F32)).astype(BF)


def dot2(a, b):
    return dotf(jnp.concatenate(split(a), 1), jnp.concatenate([b, b], 0))


def inverses(lowers, ii, jj):
    diff = lax.bitwise_xor(ii, jj)
    eye = (ii == jj).astype(F32)
    low_b = [m.astype(BF) for m in lowers]
    zero = jnp.zeros((), BF)
    inv = [eye - jnp.where(diff == 1, m, 0.0) for m in lowers]
    for b in (2, 4, 8):
        mask = (diff >= b) & (diff < 2 * b)
        cross = [jnp.where(mask, m, zero) for m in low_b]
        inv_b = [x.astype(BF) for x in inv]
        ys = [dotf(c, x).astype(BF) for c, x in zip(cross, inv_b)]
        zs = [dotf(x, y) for x, y in zip(inv_b, ys)]
        inv = [x - z for x, z in zip(inv, zs)]
    for b in (16, 32, 64):
        mask = (diff >= b) & (diff < 2 * b)

        def lower_rows(a):
            return jnp.concatenate([a[o + b : o + 2 * b] for o in range(0, C, 2 * b)], 0)

        mask_low = lower_rows(mask)
        cross = [jnp.where(mask_low, lower_rows(m), zero) for m in low_b]
        inv_b = [x.astype(BF) for x in inv]
        ys = [dotf(c, x).astype(BF) for c, x in zip(cross, inv_b)]
        pad = jnp.zeros((b, C), BF)
        full = []
        for y in ys:
            parts = []
            for k in range(C // (2 * b)):
                parts += [pad, y[k * b : (k + 1) * b]]
            full.append(jnp.concatenate(parts, 0))
        zs = [dotf(lower_rows(x), y) for x, y in zip(inv_b, full)]
        out = []
        for x, z in zip(inv, zs):
            parts = []
            for k in range(C // (2 * b)):
                o = k * 2 * b
                parts += [x[o : o + b], x[o + b : o + 2 * b] - z[k * b : (k + 1) * b]]
            out.append(jnp.concatenate(parts, 0))
        inv = out
    inv_b = [x.astype(BF) for x in inv]
    prods = [dot2(m, x) for m, x in zip(lowers, inv_b)]
    errs = [(eye - x.astype(F32) - p).astype(BF) for x, p in zip(inv_b, prods)]
    return [x.astype(F32) + dotf(x, e) for x, e in zip(inv_b, errs)]


def setup_gates(decay_t, rate_t, g_ref, b_ref, gt_ref):
    ii = lax.broadcasted_iota(jnp.int32, (C, C), 0)
    jj = lax.broadcasted_iota(jnp.int32, (C, C), 1)
    tri = (ii <= jj).astype(F32)
    for c in range(NCH):
        sl = slice(c * C, (c + 1) * C)
        gt_ref[:, sl] = jnp.dot(
            decay_t[:, sl], tri, precision=lax.Precision.HIGHEST, preferred_element_type=F32
        )
    g_ref[...] = gt_ref[...].T
    b_ref[...] = rate_t.T


def local_heads(heads, q, k, v, g_all, b_all, gt_ref, bt_ref, between):
    ii = lax.broadcasted_iota(jnp.int32, (C, C), 0)
    jj = lax.broadcasted_iota(jnp.int32, (C, C), 1)
    tri = ii >= jj
    strict = ii > jj
    eye = (ii == jj).astype(F32)
    lane = lax.broadcasted_iota(jnp.int32, g_all.shape, 1)
    kns, qs, vs, gcs, grs, brs, bcs = [], [], [], [], [], [], []
    for n, h in enumerate(heads):
        kf = k[n].astype(F32)
        kn = (kf * lax.rsqrt(jnp.sum(kf * kf, axis=-1, keepdims=True) + 1e-6)).astype(BF)
        gcol = jnp.sum(jnp.where(lane == h, g_all, 0.0), axis=1, keepdims=True)
        bcol = jnp.sum(jnp.where(lane == h, b_all, 0.0), axis=1, keepdims=True)
        grow = gt_ref[pl.ds(h, 1), :]
        brow = bt_ref[pl.ds(h, 1), :]
        for c in range(NCH):
            sl = slice(c * C, (c + 1) * C)
            kns.append(kn[sl])
            qs.append(q[n][sl])
            vs.append(v[n][sl])
            gcs.append(gcol[sl])
            bcs.append(bcol[sl])
            grs.append(grow[:, sl])
            brs.append(brow[:, sl])
    falls = [jnp.exp(jnp.where(tri, gc - gr, -1e30)) for gc, gr in zip(gcs, grs)]
    gram = [dotf(a, a, NT) for a in kns]
    qk = [dotf(a, b, NT) for a, b in zip(qs, kns)]
    lowers = [jnp.where(strict, bc * d * g, 0.0) for bc, d, g in zip(bcs, falls, gram)]
    scores = [(a * d).astype(BF) for a, d in zip(qk, falls)]
    inv = inverses(lowers, ii, jj)
    between()
    egr = [jnp.exp(g) for g in grs]
    egc = [jnp.exp(g) for g in gcs]
    wv = [dot2(x * b, vv) for x, b, vv in zip(inv, brs, vs)]
    wk = [dot2(x * (b * e), kk) for x, b, e, kk in zip(inv, brs, egr, kns)]
    count = len(heads)
    near, rows = [[] for _ in heads], [[] for _ in heads]
    pair = [None] * count
    for c in range(NCH):
        for n in range(count):
            i = n * NCH + c
            glast = gcs[i][C - 1 : C, :]
            fall = jnp.exp(glast)
            tail = jnp.exp(glast - gcs[i])
            if c == 0:
                errors = jnp.concatenate([wv[i], -wk[i]], axis=1)
            else:
                pair_b = pair[n].astype(BF)
                errors = jnp.concatenate([wv[i], jnp.zeros_like(wv[i])], axis=1) - dotf(wk[i].astype(BF), pair_b)
            mixed = dotf(scores[i], errors.astype(BF))
            if c == 0:
                near_c = mixed[:, :128]
                rows_c = egc[i] * qs[i].astype(F32) + mixed[:, 128:]
            else:
                mixed = mixed + egc[i] * dotf(qs[i], pair_b)
                near_c = mixed[:, :128]
                rows_c = mixed[:, 128:]
            near[n].append(near_c)
            rows[n].append(rows_c.astype(BF))
            grown = dotf(jnp.concatenate([kns[i], kns[i]], 0), jnp.concatenate(split(tail * errors), 0), TN)
            if c == 0:
                pair[n] = jnp.concatenate([jnp.zeros((128, 128), F32), fall * eye], axis=1) + grown
            else:
                pair[n] = fall * pair[n] + grown
    near = [jnp.concatenate(x, 0) for x in near]
    rows = [jnp.concatenate(x, 0) for x in rows]
    return near, rows, pair


MESH = pl.DeviceIdType.MESH
HEADS = 8
LEV = 4
GROUPS = ((0, 2), (2, 6), (6, 8))


def fused_kernel(
    q_hbm, k_hbm, v_hbm, ldt_ref, bt_ref, wt_ref, lev_ref, out_ref,
    q_ref, k_ref, v_ref, g_ref, b_ref, gt_ref, near_ref, rows_ref,
    box, box_s, run_f, prefix, carried, w_ref, stage,
    in_sem, send_sem, recv_sem, out_send, out_recv, own_sem,
):
    pos = lax.axis_index("ctx")
    me = lax.axis_index("head")
    bits = [(pos // 2**r) % 2 for r in range(LEV)]
    x, z = pos // 4, pos % 4
    mates = [pos + 1 - 2 * bits[0], pos + 3 - 2 * z, pos + 4 - 8 * bits[2], pos + 12 - 8 * x]
    peers = [lax.rem(me + d, HEADS) for d in range(1, HEADS)]

    barrier = pltpu.get_barrier_semaphore()
    for m in mates:
        pl.semaphore_signal(barrier, inc=1, device_id={"ctx": m}, device_id_type=MESH)
    for j in peers:
        pl.semaphore_signal(barrier, inc=1, device_id={"head": j}, device_id_type=MESH)

    def in_copies(p):
        lo, hi = GROUPS[p]
        cols = pl.ds(lo * 128, (hi - lo) * 128)
        return [
            pltpu.make_async_copy(src.at[:, cols], dst.at[:, cols], in_sem.at[i, p])
            for i, (src, dst) in enumerate(((k_hbm, k_ref), (q_hbm, q_ref), (v_hbm, v_ref)))
        ]

    for p in range(len(GROUPS)):
        for c in in_copies(p):
            c.start()

    def run_copy(r, h):
        if r == LEV - 1:
            src, dst = box_s.at[h, 0], box_s.at[h, 1]
        else:
            src, dst = box.at[r, h, 0], box.at[r, h, 1]
        return pltpu.make_async_remote_copy(
            src_ref=src,
            dst_ref=dst,
            send_sem=send_sem.at[r, h],
            recv_sem=recv_sem.at[r, h],
            device_id={"ctx": mates[r]},
            device_id_type=MESH,
        )

    def head_cols(h):
        if isinstance(h, int):
            return pl.ds(h * 128, 128)
        return pl.ds(pl.multiple_of(h * 128, 128), 128)

    def out_copy(h, src_dev, dst_dev):
        cols = pl.ds(pl.multiple_of(src_dev * 1024 + h * 128, 128), 128)
        return pltpu.make_async_remote_copy(
            src_ref=stage.at[pl.ds(pl.multiple_of(dst_dev * 64, 64), 64), head_cols(h)],
            dst_ref=out_ref.at[:, cols],
            send_sem=out_send.at[h, dst_dev],
            recv_sem=out_recv.at[h, src_dev],
            device_id={"head": dst_dev},
            device_id_type=MESH,
        )

    def own_copy(h):
        cols = pl.ds(pl.multiple_of(me * 1024 + h * 128, 128), 128)
        return pltpu.make_async_copy(
            stage.at[pl.ds(pl.multiple_of(me * 64, 64), 64), head_cols(h)], out_ref.at[:, cols], own_sem.at[h]
        )

    setup_gates(ldt_ref[...], bt_ref[...], g_ref, b_ref, gt_ref)

    lane = lax.broadcasted_iota(jnp.int32, (64, 40), 1)
    level = lane
    for m in range(1, HEADS):
        level = jnp.where(lane >= LEVELS * m, lane - LEVELS * m, level)
    w_all = wt_ref[...].T
    for n in range(8):
        sl = slice(64 * n, 64 * n + 64)
        w_ref[sl, :] = jnp.where(level < lev_ref[n], w_all[sl], 0.0)

    lanes = lax.broadcasted_iota(jnp.int32, (512, 40), 1)

    def finish(h):
        w = w_ref[...]
        weight = [
            jnp.sum(jnp.where(lanes == h * LEVELS + i, w, 0.0), axis=1, keepdims=True) for i in range(LEVELS)
        ]
        far = dotf(rows_ref[:, head_cols(h)], carried[h])
        total = weight[0] * near_ref[:, head_cols(h)]
        for i in range(LEV):
            total = total + weight[i + 1] * far[:, i * 128 : (i + 1) * 128]
        stage[:, head_cols(h)] = total.astype(BF)
        for j in peers:
            out_copy(h, me, j).start()
        own_copy(h).start()

    def step(r, h):
        up = bits[r] == 1
        run_copy(r, h).wait_recv()
        cr = slice(r * 128, (r + 1) * 128)
        if r == LEV - 1:
            far = dotf(prefix[h].astype(BF), box_s[h, 1])
            carried[h, :, cr] = jnp.where(up, far, 0.0).astype(BF)
            finish(h)
            return
        left = box[r, h, bits[r]]
        right = box[r, h, 1 - bits[r]]
        right_s = jnp.where(up, run_f[h, :, :128], right[:, :128].astype(F32))
        if r == 0:
            ii = lax.broadcasted_iota(jnp.int32, (128, 128), 0)
            jj = lax.broadcasted_iota(jnp.int32, (128, 128), 1)
            both = left.astype(F32)
            old = (ii == jj).astype(F32)
        else:
            old = prefix[h]
            both = dotf(old.astype(BF), left)
        carried[h, :, cr] = jnp.where(up, both[:, :128], 0.0).astype(BF)
        prefix[h] = jnp.where(up, both[:, 128:], old)
        if r < LEV - 2:
            joined = dotf(right[:, 128:], left)
            state = joined[:, :128] + right_s
            run_f[h] = state
            box[r + 1, h, 0, :, :128] = state.astype(BF)
            box[r + 1, h, 0, :, 128:] = joined[:, 128:].astype(BF)
        else:
            box_s[h, 0] = (dotf(right[:, 128:], left[:, :128]) + right_s).astype(BF)
        run_copy(r + 1, h).start()

    def steps(todo):
        for r, lo, hi in todo:

            @pl.loop(lo, hi)
            def _(h):
                step(r, h)

    def local_group(p, inside):
        for c in in_copies(p):
            c.wait()
        heads = list(range(*GROUPS[p]))

        def cut(ref):
            return [ref[:, head_cols(h)] for h in heads]

        near, rows, pair = local_heads(
            heads, cut(q_ref), cut(k_ref), cut(v_ref), g_ref[...], b_ref[...], gt_ref, bt_ref, lambda: steps(inside)
        )
        if p == 0:
            pl.semaphore_wait(barrier, LEV + HEADS - 1)
        for n, h in enumerate(heads):
            run_f[h] = pair[n][:, :128]
            box[0, h, 0] = pair[n].astype(BF)
            run_copy(0, h).start()
        for n, h in enumerate(heads):
            near_ref[:, head_cols(h)] = near[n]
            rows_ref[:, head_cols(h)] = rows[n]

    local_group(0, ())
    local_group(1, ((0, 0, 2),))
    steps(((1, 0, 2),))
    local_group(2, ((0, 2, 4), (2, 0, 2)))
    steps(((0, 4, 6), (1, 2, 4), (3, 0, 2), (0, 6, 8), (1, 4, 6), (2, 2, 4), (1, 6, 8), (2, 4, 6), (3, 2, 4)))
    steps(((2, 6, 8), (3, 4, 6), (3, 6, 8)))

    @pl.loop(0, HEADS)
    def _(h):
        for r in range(LEV):
            run_copy(r, h).wait_send()
        own_copy(h).wait()
        for j in peers:
            out_copy(h, me, j).wait_send()
        for j in peers:
            out_copy(h, j, me).wait_recv()


def fused_call(q, k, v, decay, rate, weights, levels_in):
    vmem = pl.BlockSpec(memory_space=pltpu.VMEM)
    hbm = pl.BlockSpec(memory_space=pl.ANY)
    return pl.pallas_call(
        fused_kernel,
        in_specs=[hbm, hbm, hbm, vmem, vmem, vmem, pl.BlockSpec(memory_space=pltpu.SMEM)],
        out_specs=hbm,
        out_shape=jax.ShapeDtypeStruct((64, 8192), BF),
        scratch_shapes=[
            pltpu.VMEM((512, 1024), BF),
            pltpu.VMEM((512, 1024), BF),
            pltpu.VMEM((512, 1024), BF),
            pltpu.VMEM((512, 8), F32),
            pltpu.VMEM((512, 8), F32),
            pltpu.VMEM((8, 512), F32),
            pltpu.VMEM((512, 1024), F32),
            pltpu.VMEM((512, 1024), BF),
            pltpu.VMEM((LEV - 1, HEADS, 2, 128, 256), BF),
            pltpu.VMEM((HEADS, 2, 128, 128), BF),
            pltpu.VMEM((HEADS, 128, 128), F32),
            pltpu.VMEM((HEADS, 128, 128), F32),
            pltpu.VMEM((HEADS, 128, LEV * 128), BF),
            pltpu.VMEM((512, 40), F32),
            pltpu.VMEM((512, 1024), BF),
            pltpu.SemaphoreType.DMA((3, len(GROUPS))),
            pltpu.SemaphoreType.DMA((LEV, HEADS)),
            pltpu.SemaphoreType.DMA((LEV, HEADS)),
            pltpu.SemaphoreType.DMA((HEADS, HEADS)),
            pltpu.SemaphoreType.DMA((HEADS, HEADS)),
            pltpu.SemaphoreType.DMA((HEADS,)),
        ],
        compiler_params=pltpu.CompilerParams(
            collective_id=0, has_side_effects=True, vmem_limit_bytes=56 << 20
        ),
        name="fused",
    )(q, k, v, decay.T, rate.T, weights.T, levels_in)


def solution(mesh):
    in_specs = (P("ctx", "head"),) * 6 + (P("ctx"),)
    out_specs = P(("ctx", "head"), None)
    return jax.shard_map(fused_call, mesh=mesh, in_specs=in_specs, out_specs=out_specs, check_vma=False)
```
